128 devices in a mesh: gx: 4 (over x), gy: 32 (over z, y, core).
Axes of the slice: x: 4, y: 4, z: 4, core: 2. Of those that a mesh axis runs over, the one named last changes fastest.
Arguments:
- starting_sag: float32 [512, 4096], P('gx', 'gy'), may hold values from -6 to 6
- warmth_celsius_field: float32 [512, 4096], P('gx', 'gy'), may hold values from 25 to 125
- junction_charge_store: float32 [512, 4096], P('gx', 'gy'), may hold values from 5e-05 to 0.0005
- load_amperes: float32 [2, 512, 4096], P(None, 'gx', 'gy'), may hold values from -0.08 to 0.08
- source_patch_bits: int32 [16, 128], P('gx', 'gy'), may hold values 0 or 1
Outputs:
- drop: float32 [512, 4096], P('gx', 'gy')
The draws below stay inside these ranges and needn't reach their ends.
All inputs are finite; a program needn't handle non-finite values. No bound on the sum of `source_patch_bits` on one device may be relied on, other than what follows from the above.
Results may differ from the reference program's by a relative error of at most 0.0013.
Values sent between devices are 32-bit elements; how exact they have to be, the bound alone decides.
No kernel may reach another device: no remote copies, remote signals or barrier semaphores. Data moves between devices by JAX's collectives and lax.ppermute only.
A program may use at most 64 MiB of HBM per device.

```python
import math
import jax
import jax.numpy as jnp
from jax import lax

STEPS = 2
PITCH = 32
POINTS_EACH_RUN = 512
STRIP_TRACKS = 4096


def draw_load_amperes(key, part):
    rough_key = jax.random.fold_in(key, 0)
    rough_part = jnp.clip(jax.random.normal(rough_key, (STEPS, POINTS_EACH_RUN, STRIP_TRACKS), jnp.float32), -6.0, 6.0) * 0.01
    return rough_part


def place_ends(values, stream_key, smallest, high):
    place = [jax.random.randint(jax.random.fold_in(stream_key, axis), (), 0, length) for axis, length in enumerate(values.shape)]
    longest = values.shape.index(max(values.shape))
    beside = place[:longest] + [(place[longest] + 1) % values.shape[longest]] + place[longest + 1:]
    return values.at[tuple(place)].set(smallest).at[tuple(beside)].set(high)


def block_levels(key, shape, cuts, low, top_value):
    level, own = 1.0, jax.random.fold_in(key, 6)
    for dim, shards_of in cuts:
        steps = jnp.exp(jax.random.uniform(jax.random.fold_in(own, dim), (shards_of,), jnp.float32, low / len(cuts), top_value / len(cuts)))
        level = level * jnp.repeat(steps, shape[dim] // shards_of).reshape([-1 if axis == dim else 1 for axis in range(len(shape))])
    return level


def noise(own_key, shape, spread, bound, cuts=(), kind=jnp.bfloat16):
    entries = jax.random.normal(own_key, shape, jnp.float32) * spread
    if len(cuts) > 0:
        entries = block_levels(own_key, shape, cuts, -0.22, 0.18) * entries
    return jnp.clip(entries, min=-bound, max=bound).astype(kind)


def setup_inputs(seed: int = 0) -> dict:
    arg_keys = jax.random.split(jax.random.key(seed), 6)
    starting_sag = noise(arg_keys[0], (POINTS_EACH_RUN, STRIP_TRACKS), 1.0, 6.0, ((0, 4), (1, 32)), jnp.float32)
    warmth_celsius_field = jnp.clip(25.0 + 100.0 * jax.random.uniform(arg_keys[1], (POINTS_EACH_RUN, STRIP_TRACKS), jnp.float32) ** block_levels(arg_keys[1], (POINTS_EACH_RUN, STRIP_TRACKS), ((0, 4), (1, 32)), -0.2, 0.2), 25.0, 125.0)
    junction_charge_store = jnp.clip(jnp.exp(math.log(0.0005) - 2.3025852 * jax.random.uniform(arg_keys[2], (POINTS_EACH_RUN, STRIP_TRACKS), jnp.float32) ** block_levels(arg_keys[2], (POINTS_EACH_RUN, STRIP_TRACKS), ((0, 4), (1, 32)), -0.2, 0.2)), 4.999999873689376e-05, 0.0005)
    load_amperes = draw_load_amperes(jax.random.fold_in(arg_keys[5], 71), 0)
    source_patch_bits = place_ends((jax.random.randint(arg_keys[4], (POINTS_EACH_RUN // PITCH, STRIP_TRACKS // PITCH), 0, 2) < 1).astype(jnp.int32), jax.random.fold_in(arg_keys[4], 1), 0, 1)
    return dict(starting_sag=starting_sag, warmth_celsius_field=warmth_celsius_field, junction_charge_store=junction_charge_store, load_amperes=load_amperes, source_patch_bits=source_patch_bits)


xward_admittance = 1.0
yward_admittance = 0.5
warmth_scaling = 0.004
surrounding_warmth = 25.0
cushion_pieces = 1.0


def factor(sub_diag, main_diag, sup_diag):
    def advance(prev_ratio, packed):
        sub_row, main_row, sup_row = packed
        pivot_row = 1.0 / (main_row - sub_row * prev_ratio)
        next_ratio = sup_row * pivot_row
        return next_ratio, (pivot_row, next_ratio)

    _, (pivots, ratios) = lax.scan(advance, jnp.zeros_like(main_diag[0]), (sub_diag, main_diag, sup_diag))
    return pivots, ratios


def substitute(sub_diag, pivots, ratios, source):
    def forward(prev_value, packed):
        sub_row, pivot_row, source_row = packed
        new_value = (source_row - sub_row * prev_value) * pivot_row
        return new_value, new_value

    _, partial_sol = lax.scan(forward, jnp.zeros_like(source[0]), (sub_diag, pivots, source))

    def backward(next_value, packed):
        ratio_row, partial_row = packed
        new_value = partial_row - ratio_row * next_value
        return new_value, new_value

    _, solved = lax.scan(backward, jnp.zeros_like(source[0]), (ratios, partial_sol), reverse=True)
    return solved


def reference(starting_sag, warmth_celsius_field, junction_charge_store, load_amperes, source_patch_bits):
    xward_wire = xward_admittance / (1.0 + warmth_scaling * (0.5 * (warmth_celsius_field[:-1] + warmth_celsius_field[1:]) - surrounding_warmth))
    yward_wire = yward_admittance / (1.0 + warmth_scaling * (0.5 * (warmth_celsius_field[:, :-1] + warmth_celsius_field[:, 1:]) - surrounding_warmth))
    blank_xcoord = jnp.zeros((1, STRIP_TRACKS), warmth_celsius_field.dtype)
    blank_ycoord = jnp.zeros((POINTS_EACH_RUN, 1), warmth_celsius_field.dtype)
    left_x = jnp.concatenate([blank_xcoord, xward_wire], 0)
    right_x = jnp.concatenate([xward_wire, blank_xcoord], 0)
    left_y = jnp.concatenate([blank_ycoord, yward_wire], 1)
    right_y = jnp.concatenate([yward_wire, blank_ycoord], 1)
    patch_indicators = jnp.repeat(jnp.repeat(source_patch_bits, PITCH, axis=0), PITCH, axis=1)
    xcoord_table = (jnp.arange(POINTS_EACH_RUN) % PITCH == 0)[:, None]
    ycoord_table = (jnp.arange(STRIP_TRACKS) % PITCH == 0)[None, :]
    semi_cushion = jnp.where(xcoord_table & ycoord_table & (patch_indicators == 1), cushion_pieces, 0.0).astype(warmth_celsius_field.dtype)
    diag_x = junction_charge_store + left_x + right_x + semi_cushion
    diag_y = junction_charge_store + left_y + right_y + semi_cushion
    pivots_x, ratios_x = factor(-left_x, diag_x, -right_x)
    pivots_y, ratios_y = factor(-left_y.T, diag_y.T, -right_y.T)

    def operate_x(field_in):
        padded = jnp.pad(field_in, ((1, 1), (0, 0)))
        return right_x * (field_in - padded[2:]) + left_x * (field_in - padded[:-2]) + semi_cushion * field_in

    def operate_y(field_in):
        padded = jnp.pad(field_in, ((0, 0), (1, 1)))
        return right_y * (field_in - padded[:, 2:]) + left_y * (field_in - padded[:, :-2]) + semi_cushion * field_in

    drop_now = starting_sag
    for step_index in range(STEPS):
        source = junction_charge_store * drop_now - operate_y(drop_now) + load_amperes[step_index]
        half_drop = substitute(-left_x, pivots_x, ratios_x, source)
        source = junction_charge_store * half_drop - operate_x(half_drop) + load_amperes[step_index]
        drop_now = substitute(-left_y.T, pivots_y, ratios_y, source.T).T
    return drop_now
```

```python
import jax
import jax.numpy as jnp
from jax import lax
from jax.experimental import pallas as pl
from jax.experimental.pallas import tpu as pltpu
from jax.sharding import PartitionSpec as P

PITCH = 32
xward_admittance = 1.0
yward_admittance = 0.5
warmth_scaling = 0.004
surrounding_warmth = 25.0
cushion_pieces = 1.0

SUB = 8
LANES = 128
ROWS = 128
DEPTH = ROWS // SUB
COUNT_X = 4
COUNT_Y = 32
Y_DEPTH = COUNT_Y // SUB

INNER = (
    [(m, m - 1, m + 1) for m in range(1, DEPTH - 2, 2)]
    + [(2, 0, 4), (6, 4, 8), (10, 8, 12), (14, 12, 15)]
    + [(4, 0, 8), (12, 8, 15), (8, 0, 15)]
)
SPANS = (1, 2, 4)
LOCAL_COEFS = 3 * (len(INNER) + 1 + len(SPANS))

def path_order(nodes):
    order = []
    while len(nodes) > 1:
        for at in range(1, len(nodes), 2):
            right = nodes[at + 1] if at + 1 < len(nodes) else None
            order.append((nodes[at], nodes[at - 1], right))
        nodes = nodes[::2]
    return order + [(nodes[0], None, None)]


X_ORDER = path_order(list(range(2 * COUNT_X)))
X_COEFS = 3 * len(X_ORDER)
Y_ORDER = [(1, 0, 2), (3, 2, 4), (5, 4, 6), (7, 6, 8), (2, 0, 4), (6, 4, 8), (4, 0, 8)]
Y_COEFS = 3 * (len(Y_ORDER) + len(SPANS)) + 1


def wire(admittance, warm_a, warm_b):
    return admittance / (1.0 + warmth_scaling * (0.5 * (warm_a + warm_b) - surrounding_warmth))


def sublanes():
    return lax.broadcasted_iota(jnp.int32, (SUB, LANES), 0)


def roll(x, by):
    return pltpu.roll(x, by % SUB, 0)


def spread(row):
    return jnp.broadcast_to(row, (SUB, LANES))


def load_lines(ref):
    return [ref[pl.ds(r, SUB, stride=DEPTH), :] for r in range(DEPTH)]


def store_lines(ref, values):
    for r in range(DEPTH):
        ref[pl.ds(r, SUB, stride=DEPTH), :] = values[r]


def load_regs(ref, count=DEPTH):
    return [ref[pl.ds(SUB * r, SUB), :] for r in range(count)]


def store_regs(ref, values):
    for r, value in enumerate(values):
        ref[pl.ds(SUB * r, SUB), :] = value


def coef(ref, k):
    return [ref[pl.ds(SUB * (3 * k + n), SUB), :] for n in range(3)]


def put_coef(ref, k, values):
    for n, value in enumerate(values):
        ref[pl.ds(SUB * (3 * k + n), SUB), :] = value


def factor_local(ref, ground, edges, across):
    sub = sublanes()
    edges = dict(edges)
    for k, (m, left, right) in enumerate(INNER):
        to_left, to_right = edges[(left, m)], edges[(m, right)]
        inverse = 1.0 / (to_left + to_right + ground[m])
        by_left, by_right = to_left * inverse, to_right * inverse
        ground[left] = ground[left] + by_left * ground[m]
        ground[right] = ground[right] + by_right * ground[m]
        edges[(left, right)] = to_left * by_right
        put_coef(ref, k, (inverse, by_left, by_right))
    own, first, last = edges[(0, DEPTH - 1)], ground[0], ground[DEPTH - 1]
    inside = sub < SUB - 1
    inverse = jnp.where(inside, 1.0 / (own + across + last), 0.0)
    by_left, by_right = own * inverse, across * inverse
    put_coef(ref, len(INNER), (inverse, by_left, by_right))
    edge = jnp.where(inside, own * by_right, own)
    end = roll(last, 1)
    first = first + by_left * last + roll(by_right * last, 1)
    for n, span in enumerate(SPANS):
        chosen = sub % (2 * span) == span
        to_left = roll(edge, span)
        inverse = jnp.where(chosen, 1.0 / (to_left + edge + first), 0.0)
        by_left, by_right = to_left * inverse, edge * inverse
        put_coef(ref, len(INNER) + 1 + n, (inverse, by_left, by_right))
        passed = roll(by_right * first, span)
        end = end + passed
        first = first + roll(by_left * first, -span) + jnp.where(sub == 0, 0.0, passed)
        edge = roll(to_left * by_right, -span)
    return edge[0:1], first[0:1], end[0:1]


def forward_local(ref, f):
    sub = sublanes()
    for k, (m, left, right) in enumerate(INNER):
        _, by_left, by_right = coef(ref, k)
        f[left] = f[left] + by_left * f[m]
        f[right] = f[right] + by_right * f[m]
    first, last = f[0], f[DEPTH - 1]
    _, by_left, by_right = coef(ref, len(INNER))
    end = roll(last, 1)
    first = first + by_left * last + roll(by_right * last, 1)
    for n, span in enumerate(SPANS):
        _, by_left, by_right = coef(ref, len(INNER) + 1 + n)
        passed = roll(by_right * first, span)
        end = end + passed
        first = first + roll(by_left * first, -span) + jnp.where(sub == 0, 0.0, passed)
    f[0] = first
    return first[0:1], end[0:1]


def backward_local(ref, f, first, end):
    sub = sublanes()
    x = jnp.where(sub == 0, first, 0.0)
    for n in range(len(SPANS) - 1, -1, -1):
        span = SPANS[n]
        inverse, by_left, by_right = coef(ref, len(INNER) + 1 + n)
        beyond = roll(jnp.where(sub == 0, end, x), -span)
        found = inverse * f[0] + by_left * roll(x, span) + by_right * beyond
        x = jnp.where(sub % (2 * span) == span, found, x)
    inverse, by_left, by_right = coef(ref, len(INNER))
    found = inverse * f[DEPTH - 1] + by_left * x + by_right * roll(x, -1)
    out = [None] * DEPTH
    out[0] = x
    out[DEPTH - 1] = jnp.where(sub == SUB - 1, end, found)
    for k in range(len(INNER) - 1, -1, -1):
        m, left, right = INNER[k]
        inverse, by_left, by_right = coef(ref, k)
        out[m] = inverse * f[m] + by_left * out[left] + by_right * out[right]
    return out


def put_rows(ref, rows):
    for n, row in enumerate(rows):
        ref[n : n + 1, :] = row


def gather_x(joined, own, others):
    place = lax.axis_index("gx")
    count = own.shape[0]
    joined[pl.ds(pl.multiple_of(place * SUB, SUB), count), :] = own[...]
    for n, other in enumerate(others):
        source = lax.rem(place + COUNT_X - (n + 1), COUNT_X)
        joined[pl.ds(pl.multiple_of(source * SUB, SUB), count), :] = other[...]


def factor_x(ref, joined):
    def row(p, q):
        return spread(joined[SUB * p + q : SUB * p + q + 1, :])

    ground, edges = {}, {}
    for p in range(COUNT_X):
        ground[2 * p], ground[2 * p + 1] = row(p, 2), row(p, 3)
        edges[(2 * p, 2 * p + 1)] = row(p, 4)
        if p + 1 < COUNT_X:
            edges[(2 * p + 1, 2 * p + 2)] = wire(xward_admittance, row(p, 6), row(p + 1, 5))
    for k, (m, left, right) in enumerate(X_ORDER):
        total = ground[m]
        if left is not None:
            total = total + edges[(left, m)]
        if right is not None:
            total = total + edges[(m, right)]
        inverse = 1.0 / total
        by_left = edges[(left, m)] * inverse if left is not None else inverse
        by_right = edges[(m, right)] * inverse if right is not None else inverse
        if left is not None:
            ground[left] = ground[left] + by_left * ground[m]
        if right is not None:
            ground[right] = ground[right] + by_right * ground[m]
        if left is not None and right is not None:
            edges[(left, right)] = edges[(left, m)] * by_right
        put_coef(ref, k, (inverse, by_left, by_right))


def solve_x(ref, joined):
    f = [
        spread(joined[SUB * (n // 2) + n % 2 : SUB * (n // 2) + n % 2 + 1, :])
        for n in range(2 * COUNT_X)
    ]
    for k, (m, left, right) in enumerate(X_ORDER):
        _, by_left, by_right = coef(ref, k)
        if left is not None:
            f[left] = f[left] + by_left * f[m]
        if right is not None:
            f[right] = f[right] + by_right * f[m]
    x = [None] * len(f)
    for k in range(len(X_ORDER) - 1, -1, -1):
        m, left, right = X_ORDER[k]
        inverse, by_left, by_right = coef(ref, k)
        x[m] = inverse * f[m]
        if left is not None:
            x[m] = x[m] + by_left * x[left]
        if right is not None:
            x[m] = x[m] + by_right * x[right]
    place = lax.axis_index("gx")
    first, end = x[0], x[1]
    for p in range(1, COUNT_X):
        first = jnp.where(place == p, x[2 * p], first)
        end = jnp.where(place == p, x[2 * p + 1], end)
    return first, end


def factor_y(ref, joined):
    sub = sublanes()

    def part(r, q):
        return joined[pl.ds(SUB * r + q, SUB, stride=SUB * Y_DEPTH), :]

    ground, edges = {}, {}
    for r in range(Y_DEPTH):
        ground[2 * r], ground[2 * r + 1] = part(r, 2), part(r, 3)
        edges[(2 * r, 2 * r + 1)], edges[(2 * r + 1, 2 * r + 2)] = part(r, 4), part(r, 5)
    last = 2 * Y_DEPTH
    for k, (m, left, right) in enumerate(Y_ORDER):
        to_left, to_right = edges[(left, m)], edges[(m, right)]
        inverse = 1.0 / (to_left + to_right + ground[m])
        by_left, by_right = to_left * inverse, to_right * inverse
        put_coef(ref, k, (inverse, by_left, by_right))
        ground[left] = ground[left] + by_left * ground[m]
        passed = by_right * ground[m]
        if right == last:
            ground[0] = ground[0] + roll(passed, 1)
        else:
            ground[right] = ground[right] + passed
        edges[(left, right)] = to_left * by_right
    edge, first = edges[(0, last)], ground[0]
    for n, span in enumerate(SPANS):
        chosen = sub % (2 * span) == span
        to_left = roll(edge, span)
        inverse = jnp.where(chosen, 1.0 / (to_left + edge + first), 0.0)
        by_left, by_right = to_left * inverse, edge * inverse
        put_coef(ref, len(Y_ORDER) + n, (inverse, by_left, by_right))
        first = first + roll(by_left * first, -span) + roll(by_right * first, span)
        edge = roll(to_left * by_right, -span)
    ref[pl.ds(SUB * (Y_COEFS - 1), SUB), :] = jnp.where(sub == 0, 1.0 / first, 0.0)


def solve_y(ref, joined, stride, found):
    sub = sublanes()
    last = 2 * Y_DEPTH
    f = [
        joined[pl.ds(stride * (n // 2) + n % 2, SUB, stride=stride * Y_DEPTH), :]
        for n in range(last)
    ]
    for k, (m, left, right) in enumerate(Y_ORDER):
        _, by_left, by_right = coef(ref, k)
        f[left] = f[left] + by_left * f[m]
        if right == last:
            f[0] = f[0] + roll(by_right * f[m], 1)
        else:
            f[right] = f[right] + by_right * f[m]
    first = f[0]
    for n, span in enumerate(SPANS):
        _, by_left, by_right = coef(ref, len(Y_ORDER) + n)
        first = first + roll(by_left * first, -span) + roll(by_right * first, span)
    x0 = ref[pl.ds(SUB * (Y_COEFS - 1), SUB), :] * first
    for n in range(len(SPANS) - 1, -1, -1):
        span = SPANS[n]
        inverse, by_left, by_right = coef(ref, len(Y_ORDER) + n)
        value = inverse * first + by_left * roll(x0, span) + by_right * roll(x0, -span)
        x0 = jnp.where(sub % (2 * span) == span, value, x0)
    x = [x0] + [None] * (last - 1) + [roll(x0, -1)]
    for k in range(len(Y_ORDER) - 1, -1, -1):
        m, left, right = Y_ORDER[k]
        inverse, by_left, by_right = coef(ref, k)
        x[m] = inverse * f[m] + by_left * x[left] + by_right * x[right]
    store_regs(found, x[:last])
    place = lax.axis_index("gy")
    at = lax.rem(place, Y_DEPTH) * (2 * SUB) + lax.div(place, Y_DEPTH)
    return spread(found[pl.ds(at, 1), :]), spread(found[pl.ds(at + SUB, 1), :])


def prepare(v, warm, v_t, warm_t, inside, outside):
    v_t[...] = v[...].T
    warm_t[...] = warm[...].T
    odd = lax.rem(lax.axis_index("gy"), 2) == 1
    for n, ref in enumerate((v_t, warm_t)):
        low, high = ref[0:1, :], ref[ROWS - 1 : ROWS, :]
        inside[n : n + 1, :] = jnp.where(odd, low, high)
        outside[n : n + 1, :] = jnp.where(odd, high, low)


def pads(flags, transposed):
    sub = sublanes()
    lane = lax.broadcasted_iota(jnp.int32, (SUB, LANES), 1)
    out = jnp.zeros((SUB, LANES), jnp.float32)
    for a in range(ROWS // PITCH):
        for b in range(LANES // PITCH):
            flag = flags[b, a] if transposed else flags[a, b]
            here = (sub == a * (PITCH // DEPTH)) & (lane == b * PITCH)
            out = jnp.where(here & (flag == 1), cushion_pieces, out)
    return out


def coefficients(cap, warm, warm_t, flags, x_ref, y_ref, cap_t, x_rows, y_rows, y_edges, y_pad):
    cap_t[...] = cap[...].T
    for transposed, caps, warms, ref, rows in (
        (False, cap, warm, x_ref, x_rows),
        (True, cap_t, warm_t, y_ref, y_rows),
    ):
        admittance = yward_admittance if transposed else xward_admittance
        temps = load_lines(warms)
        edges = {(r, r + 1): wire(admittance, temps[r], temps[r + 1]) for r in range(DEPTH - 1)}
        across = wire(admittance, temps[DEPTH - 1], roll(temps[0], -1))
        pad = pads(flags, transposed)
        if transposed:
            store_regs(y_edges, [edges[(r, r + 1)] for r in range(DEPTH - 1)] + [across])
            y_pad[...] = pad
        ground = load_lines(caps)
        ground[0] = ground[0] + pad
        own, first, end = factor_local(ref, ground, edges, across)
        rows[...] = jnp.zeros((SUB, LANES), jnp.float32)
        rows[2:3, :] = first
        rows[3:4, :] = end
        rows[4:5, :] = own
        if not transposed:
            rows[5:6, :] = warms[0:1, :]
            rows[6:7, :] = warms[ROWS - 1 : ROWS, :]


def begin(
    v_t, warm_t, cap_t, load, inside, outside, y_edges, y_pad, y_rows, x_ref, x_rows,
    s_out, f_out, sent, y_rows_out, flat,
):
    sub = sublanes()
    place = lax.axis_index("gy")
    odd = lax.rem(place, 2) == 1
    low_v = jnp.where(odd, inside[0:1, :], outside[0:1, :])
    low_warm = jnp.where(odd, inside[1:2, :], outside[1:2, :])
    high_v = jnp.where(odd, outside[0:1, :], inside[0:1, :])
    high_warm = jnp.where(odd, outside[1:2, :], inside[1:2, :])
    low_edge = wire(yward_admittance, low_warm, warm_t[0:1, :])
    high_edge = wire(yward_admittance, warm_t[ROWS - 1 : ROWS, :], high_warm)
    low_edge = jnp.where(place > 0, low_edge, 0.0)
    high_edge = jnp.where(place < COUNT_Y - 1, high_edge, 0.0)
    y_rows_out[...] = y_rows[...]
    y_rows_out[5:6, :] = high_edge
    v = load_lines(v_t)
    cap = load_lines(cap_t)
    edges = load_regs(y_edges)
    before = jnp.where(sub == 0, spread(low_v), roll(v[DEPTH - 1], 1))
    before_edge = jnp.where(sub == 0, spread(low_edge), roll(edges[DEPTH - 1], 1))
    after = jnp.where(sub == SUB - 1, spread(high_v), roll(v[0], -1))
    edges[DEPTH - 1] = jnp.where(sub == SUB - 1, spread(high_edge), edges[DEPTH - 1])
    flow = before_edge * (before - v[0])
    out = []
    for r in range(DEPTH):
        onward = edges[r] * ((v[r + 1] if r + 1 < DEPTH else after) - v[r])
        own = cap[r] * v[r]
        if r == 0:
            own = own - y_pad[...] * v[r]
        out.append(own + (flow + onward))
        flow = -onward
    store_lines(flat, out)
    flat[...] = flat[...].T + load[0]
    s = load_lines(flat)
    store_regs(s_out, s)
    first, end = forward_local(x_ref, s)
    store_regs(f_out, s)
    sent[...] = x_rows[...]
    sent[0:1, :] = first
    sent[1:2, :] = end


def across_x(
    own, one, two, three, cap, load, step, s_in, f_in, x_ref, y_ref, x_join, s_out, f_out, joined, flat
):
    first, end = solve_x(x_join, joined)
    half = backward_local(x_ref, load_regs(f_in), first, end)
    caps, source = load_lines(cap), load_regs(s_in)
    loads = load_lines(load.at[step])
    store_lines(
        flat, [2.0 * caps[r] * half[r] - source[r] + loads[r] for r in range(DEPTH)]
    )
    flat[...] = flat[...].T
    s = load_lines(flat)
    if s_out is not None:
        store_regs(s_out, s)
    ends = forward_local(y_ref, s)
    store_regs(f_out, s)
    return ends


def first_x(
    own, one, two, three, cap, load, s_in, f_in, x_ref, y_ref, y_rows,
    x_join, s_out, f_out, sent, joined, flat,
):
    gather_x(joined, own, (one, two, three))
    factor_x(x_join, joined)
    first, end = across_x(
        own, one, two, three, cap, load, 0, s_in, f_in, x_ref, y_ref, x_join, s_out, f_out, joined, flat
    )
    sent[...] = y_rows[...]
    sent[0:1, :] = first
    sent[1:2, :] = end


def second_x(
    own, one, two, three, cap, load, s_in, f_in, x_ref, y_ref, x_join, f_out, sent, joined, flat
):
    gather_x(joined, own, (one, two, three))
    first, end = across_x(
        own, one, two, three, cap, load, 1, s_in, f_in, x_ref, y_ref, x_join, None, f_out, joined, flat
    )
    sent[0:1, :] = first
    sent[1:2, :] = end


def first_y(
    joined, cap_t, load, s_in, f_in, y_ref, x_ref, y_join, s_out, f_out, sent, found, flat
):
    factor_y(y_join, joined)
    first, end = solve_y(y_join, joined, SUB, found)
    drop = backward_local(y_ref, load_regs(f_in), first, end)
    caps, source = load_lines(cap_t), load_regs(s_in)
    store_lines(flat, [2.0 * caps[r] * drop[r] - source[r] for r in range(DEPTH)])
    flat[...] = flat[...].T + load[1]
    s = load_lines(flat)
    store_regs(s_out, s)
    first, end = forward_local(x_ref, s)
    store_regs(f_out, s)
    sent[0:1, :] = first
    sent[1:2, :] = end


def second_y(joined, f_in, y_ref, y_join, out, found, flat):
    first, end = solve_y(y_join, joined, 2, found)
    store_lines(flat, backward_local(y_ref, load_regs(f_in), first, end))
    out[...] = flat[...].T


def call(body, shapes, args, scratch=(), scalars=()):
    specs = [
        pl.BlockSpec(memory_space=pltpu.SMEM if n in scalars else pltpu.VMEM)
        for n in range(len(args))
    ]
    return pl.pallas_call(
        body,
        out_shape=[jax.ShapeDtypeStruct((rows, LANES), jnp.float32) for rows in shapes],
        in_specs=specs,
        out_specs=[pl.BlockSpec(memory_space=pltpu.VMEM)] * len(shapes),
        scratch_shapes=[pltpu.VMEM((rows, LANES), jnp.float32) for rows in scratch],
        name=body.__name__,
    )(*args)


def share_x(sent):
    return [
        lax.ppermute(sent, "gx", [(i, (i + by) % COUNT_X) for i in range(COUNT_X)])
        for by in range(1, COUNT_X)
    ]


def share_y(sent):
    rows = sent.shape[0]
    copies = jnp.broadcast_to(sent[None], (COUNT_Y, rows, LANES))
    return lax.all_to_all(copies, "gy", split_axis=0, concat_axis=0, tiled=True).reshape(
        COUNT_Y * rows, LANES
    )


def local(starting_sag, warmth_celsius_field, junction_charge_store, load_amperes, source_patch_bits):
    v, warm, cap, load = starting_sag, warmth_celsius_field, junction_charge_store, load_amperes
    v_t, warm_t, inside, outside = call(prepare, (ROWS, ROWS, 2, 2), (v, warm))
    inside = lax.ppermute(inside, "gy", [(i, i ^ 1) for i in range(COUNT_Y)])
    pairs = [(i, (i + 1) % COUNT_Y if i % 2 else (i - 1) % COUNT_Y) for i in range(COUNT_Y)]
    outside = lax.ppermute(outside, "gy", pairs)
    coefs = SUB * LOCAL_COEFS
    x_ref, y_ref, cap_t, x_rows, y_rows, y_edges, y_pad = call(
        coefficients,
        (coefs, coefs, ROWS, SUB, SUB, ROWS, SUB),
        (cap, warm, warm_t, source_patch_bits),
        scalars=(3,),
    )
    s, f, sent, y_rows = call(
        begin,
        (ROWS, ROWS, SUB, SUB),
        (v_t, warm_t, cap_t, load, inside, outside, y_edges, y_pad, y_rows, x_ref, x_rows),
        scratch=(ROWS,),
    )
    joined = COUNT_X * SUB
    x_join, s, f, sent = call(
        first_x,
        (SUB * X_COEFS, ROWS, ROWS, SUB),
        (sent, *share_x(sent), cap, load, s, f, x_ref, y_ref, y_rows),
        scratch=(joined, ROWS),
    )
    y_join, s, f, sent = call(
        first_y,
        (SUB * Y_COEFS, ROWS, ROWS, 2),
        (share_y(sent), cap_t, load, s, f, y_ref, x_ref),
        scratch=(2 * Y_DEPTH * SUB, ROWS),
    )
    f, sent = call(
        second_x,
        (ROWS, 2),
        (sent, *share_x(sent), cap, load, s, f, x_ref, y_ref, x_join),
        scratch=(joined, ROWS),
    )
    (drop,) = call(
        second_y,
        (ROWS,),
        (share_y(sent), f, y_ref, y_join),
        scratch=(2 * Y_DEPTH * SUB, ROWS),
    )
    return drop


def solution(mesh):
    return jax.shard_map(
        local,
        mesh=mesh,
        in_specs=(P("gx", "gy"), P("gx", "gy"), P("gx", "gy"), P(None, "gx", "gy"), P("gx", "gy")),
        out_specs=P("gx", "gy"),
        check_vma=False,
    )
```

```python
import jax
import jax.numpy as jnp
from jax import lax
from jax.experimental import pallas as pl
from jax.experimental.pallas import tpu as pltpu
from jax.sharding import PartitionSpec as P

PITCH = 32
xward_admittance = 1.0
yward_admittance = 0.5
warmth_scaling = 0.004
surrounding_warmth = 25.0
cushion_pieces = 1.0

SUB = 8
LANES = 128
ROWS = 128
DEPTH = ROWS // SUB
COUNT_X = 4
COUNT_Y = 32
Y_DEPTH = COUNT_Y // SUB

INNER = (
    [(m, m - 1, m + 1) for m in range(1, DEPTH - 2, 2)]
    + [(2, 0, 4), (6, 4, 8), (10, 8, 12), (14, 12, 15)]
    + [(4, 0, 8), (12, 8, 15), (8, 0, 15)]
)
SPANS = (1, 2, 4)
LOCAL_COEFS = 3 * (len(INNER) + 1 + len(SPANS))

def path_order(nodes):
    order = []
    while len(nodes) > 1:
        for at in range(1, len(nodes), 2):
            right = nodes[at + 1] if at + 1 < len(nodes) else None
            order.append((nodes[at], nodes[at - 1], right))
        nodes = nodes[::2]
    return order + [(nodes[0], None, None)]


X_ORDER = path_order(list(range(2 * COUNT_X)))
X_COEFS = 3 * len(X_ORDER)
Y_ORDER = [(1, 0, 2), (3, 2, 4), (5, 4, 6), (7, 6, 8), (2, 0, 4), (6, 4, 8), (4, 0, 8)]
Y_COEFS = 3 * (len(Y_ORDER) + len(SPANS)) + 1


def wire(admittance, warm_a, warm_b):
    return admittance / (1.0 + warmth_scaling * (0.5 * (warm_a + warm_b) - surrounding_warmth))


def sublanes():
    return lax.broadcasted_iota(jnp.int32, (SUB, LANES), 0)


def roll(x, by):
    return pltpu.roll(x, by % SUB, 0)


def spread(row):
    return jnp.broadcast_to(row, (SUB, LANES))


def load_lines(ref):
    return [ref[pl.ds(r, SUB, stride=DEPTH), :] for r in range(DEPTH)]


def store_lines(ref, values):
    for r in range(DEPTH):
        ref[pl.ds(r, SUB, stride=DEPTH), :] = values[r]


def load_regs(ref, count=DEPTH):
    return [ref[pl.ds(SUB * r, SUB), :] for r in range(count)]


def store_regs(ref, values):
    for r, value in enumerate(values):
        ref[pl.ds(SUB * r, SUB), :] = value


def coef(ref, k):
    return [ref[pl.ds(SUB * (3 * k + n), SUB), :] for n in range(3)]


def put_coef(ref, k, values):
    for n, value in enumerate(values):
        ref[pl.ds(SUB * (3 * k + n), SUB), :] = value


def factor_local(ref, ground, edges, across):
    sub = sublanes()
    edges = dict(edges)
    for k, (m, left, right) in enumerate(INNER):
        to_left, to_right = edges[(left, m)], edges[(m, right)]
        inverse = 1.0 / (to_left + to_right + ground[m])
        by_left, by_right = to_left * inverse, to_right * inverse
        ground[left] = ground[left] + by_left * ground[m]
        ground[right] = ground[right] + by_right * ground[m]
        edges[(left, right)] = to_left * by_right
        put_coef(ref, k, (inverse, by_left, by_right))
    own, first, last = edges[(0, DEPTH - 1)], ground[0], ground[DEPTH - 1]
    inside = sub < SUB - 1
    inverse = jnp.where(inside, 1.0 / (own + across + last), 0.0)
    by_left, by_right = own * inverse, across * inverse
    put_coef(ref, len(INNER), (inverse, by_left, by_right))
    edge = jnp.where(inside, own * by_right, own)
    end = roll(last, 1)
    first = first + by_left * last + roll(by_right * last, 1)
    for n, span in enumerate(SPANS):
        chosen = sub % (2 * span) == span
        to_left = roll(edge, span)
        inverse = jnp.where(chosen, 1.0 / (to_left + edge + first), 0.0)
        by_left, by_right = to_left * inverse, edge * inverse
        put_coef(ref, len(INNER) + 1 + n, (inverse, by_left, by_right))
        passed = roll(by_right * first, span)
        end = end + passed
        first = first + roll(by_left * first, -span) + jnp.where(sub == 0, 0.0, passed)
        edge = roll(to_left * by_right, -span)
    return edge[0:1], first[0:1], end[0:1]


def forward_local(ref, f):
    sub = sublanes()
    for k, (m, left, right) in enumerate(INNER):
        _, by_left, by_right = coef(ref, k)
        f[left] = f[left] + by_left * f[m]
        f[right] = f[right] + by_right * f[m]
    first, last = f[0], f[DEPTH - 1]
    _, by_left, by_right = coef(ref, len(INNER))
    end = roll(last, 1)
    first = first + by_left * last + roll(by_right * last, 1)
    for n, span in enumerate(SPANS):
        _, by_left, by_right = coef(ref, len(INNER) + 1 + n)
        passed = roll(by_right * first, span)
        end = end + passed
        first = first + roll(by_left * first, -span) + jnp.where(sub == 0, 0.0, passed)
    f[0] = first
    return first[0:1], end[0:1]


def backward_local(ref, f, first, end):
    sub = sublanes()
    x = jnp.where(sub == 0, first, 0.0)
    for n in range(len(SPANS) - 1, -1, -1):
        span = SPANS[n]
        inverse, by_left, by_right = coef(ref, len(INNER) + 1 + n)
        beyond = roll(jnp.where(sub == 0, end, x), -span)
        found = inverse * f[0] + by_left * roll(x, span) + by_right * beyond
        x = jnp.where(sub % (2 * span) == span, found, x)
    inverse, by_left, by_right = coef(ref, len(INNER))
    found = inverse * f[DEPTH - 1] + by_left * x + by_right * roll(x, -1)
    out = [None] * DEPTH
    out[0] = x
    out[DEPTH - 1] = jnp.where(sub == SUB - 1, end, found)
    for k in range(len(INNER) - 1, -1, -1):
        m, left, right = INNER[k]
        inverse, by_left, by_right = coef(ref, k)
        out[m] = inverse * f[m] + by_left * out[left] + by_right * out[right]
    return out


def put_rows(ref, rows):
    for n, row in enumerate(rows):
        ref[n : n + 1, :] = row


def gather_x(joined, own, others):
    place = lax.axis_index("gx")
    count = own.shape[0]
    joined[pl.ds(pl.multiple_of(place * SUB, SUB), count), :] = own[...]
    for n, other in enumerate(others):
        source = lax.rem(place + COUNT_X - (n + 1), COUNT_X)
        joined[pl.ds(pl.multiple_of(source * SUB, SUB), count), :] = other[...]


def factor_x(ref, joined):
    def row(p, q):
        return spread(joined[SUB * p + q : SUB * p + q + 1, :])

    ground, edges = {}, {}
    for p in range(COUNT_X):
        ground[2 * p], ground[2 * p + 1] = row(p, 2), row(p, 3)
        edges[(2 * p, 2 * p + 1)] = row(p, 4)
        if p + 1 < COUNT_X:
            edges[(2 * p + 1, 2 * p + 2)] = wire(xward_admittance, row(p, 6), row(p + 1, 5))
    for k, (m, left, right) in enumerate(X_ORDER):
        total = ground[m]
        if left is not None:
            total = total + edges[(left, m)]
        if right is not None:
            total = total + edges[(m, right)]
        inverse = 1.0 / total
        by_left = edges[(left, m)] * inverse if left is not None else inverse
        by_right = edges[(m, right)] * inverse if right is not None else inverse
        if left is not None:
            ground[left] = ground[left] + by_left * ground[m]
        if right is not None:
            ground[right] = ground[right] + by_right * ground[m]
        if left is not None and right is not None:
            edges[(left, right)] = edges[(left, m)] * by_right
        put_coef(ref, k, (inverse, by_left, by_right))


def solve_x(ref, joined):
    f = [
        spread(joined[SUB * (n // 2) + n % 2 : SUB * (n // 2) + n % 2 + 1, :])
        for n in range(2 * COUNT_X)
    ]
    for k, (m, left, right) in enumerate(X_ORDER):
        _, by_left, by_right = coef(ref, k)
        if left is not None:
            f[left] = f[left] + by_left * f[m]
        if right is not None:
            f[right] = f[right] + by_right * f[m]
    x = [None] * len(f)
    for k in range(len(X_ORDER) - 1, -1, -1):
        m, left, right = X_ORDER[k]
        inverse, by_left, by_right = coef(ref, k)
        x[m] = inverse * f[m]
        if left is not None:
            x[m] = x[m] + by_left * x[left]
        if right is not None:
            x[m] = x[m] + by_right * x[right]
    place = lax.axis_index("gx")
    first, end = x[0], x[1]
    for p in range(1, COUNT_X):
        first = jnp.where(place == p, x[2 * p], first)
        end = jnp.where(place == p, x[2 * p + 1], end)
    return first, end


def factor_y(ref, joined):
    sub = sublanes()

    def part(r, q):
        return joined[pl.ds(SUB * r + q, SUB, stride=SUB * Y_DEPTH), :]

    ground, edges = {}, {}
    for r in range(Y_DEPTH):
        ground[2 * r], ground[2 * r + 1] = part(r, 2), part(r, 3)
        edges[(2 * r, 2 * r + 1)], edges[(2 * r + 1, 2 * r + 2)] = part(r, 4), part(r, 5)
    last = 2 * Y_DEPTH
    for k, (m, left, right) in enumerate(Y_ORDER):
        to_left, to_right = edges[(left, m)], edges[(m, right)]
        inverse = 1.0 / (to_left + to_right + ground[m])
        by_left, by_right = to_left * inverse, to_right * inverse
        put_coef(ref, k, (inverse, by_left, by_right))
        ground[left] = ground[left] + by_left * ground[m]
        passed = by_right * ground[m]
        if right == last:
            ground[0] = ground[0] + roll(passed, 1)
        else:
            ground[right] = ground[right] + passed
        edges[(left, right)] = to_left * by_right
    edge, first = edges[(0, last)], ground[0]
    for n, span in enumerate(SPANS):
        chosen = sub % (2 * span) == span
        to_left = roll(edge, span)
        inverse = jnp.where(chosen, 1.0 / (to_left + edge + first), 0.0)
        by_left, by_right = to_left * inverse, edge * inverse
        put_coef(ref, len(Y_ORDER) + n, (inverse, by_left, by_right))
        first = first + roll(by_left * first, -span) + roll(by_right * first, span)
        edge = roll(to_left * by_right, -span)
    ref[pl.ds(SUB * (Y_COEFS - 1), SUB), :] = jnp.where(sub == 0, 1.0 / first, 0.0)


def solve_y(ref, joined, stride, found):
    sub = sublanes()
    last = 2 * Y_DEPTH
    f = [
        joined[pl.ds(stride * (n // 2) + n % 2, SUB, stride=stride * Y_DEPTH), :]
        for n in range(last)
    ]
    for k, (m, left, right) in enumerate(Y_ORDER):
        _, by_left, by_right = coef(ref, k)
        f[left] = f[left] + by_left * f[m]
        if right == last:
            f[0] = f[0] + roll(by_right * f[m], 1)
        else:
            f[right] = f[right] + by_right * f[m]
    first = f[0]
    for n, span in enumerate(SPANS):
        _, by_left, by_right = coef(ref, len(Y_ORDER) + n)
        first = first + roll(by_left * first, -span) + roll(by_right * first, span)
    x0 = ref[pl.ds(SUB * (Y_COEFS - 1), SUB), :] * first
    for n in range(len(SPANS) - 1, -1, -1):
        span = SPANS[n]
        inverse, by_left, by_right = coef(ref, len(Y_ORDER) + n)
        value = inverse * first + by_left * roll(x0, span) + by_right * roll(x0, -span)
        x0 = jnp.where(sub % (2 * span) == span, value, x0)
    x = [x0] + [None] * (last - 1) + [roll(x0, -1)]
    for k in range(len(Y_ORDER) - 1, -1, -1):
        m, left, right = Y_ORDER[k]
        inverse, by_left, by_right = coef(ref, k)
        x[m] = inverse * f[m] + by_left * x[left] + by_right * x[right]
    store_regs(found, x[:last])
    place = lax.axis_index("gy")
    at = lax.rem(place, Y_DEPTH) * (2 * SUB) + lax.div(place, Y_DEPTH)
    return spread(found[pl.ds(at, 1), :]), spread(found[pl.ds(at + SUB, 1), :])


def prepare(v, warm, v_t, warm_t, inside, outside):
    v_t[...] = v[...].T
    warm_t[...] = warm[...].T
    odd = lax.rem(lax.axis_index("gy"), 2) == 1
    for n, ref in enumerate((v_t, warm_t)):
        low, high = ref[0:1, :], ref[ROWS - 1 : ROWS, :]
        inside[n : n + 1, :] = jnp.where(odd, low, high)
        outside[n : n + 1, :] = jnp.where(odd, high, low)


def pads(flags, transposed):
    sub = sublanes()
    lane = lax.broadcasted_iota(jnp.int32, (SUB, LANES), 1)
    out = jnp.zeros((SUB, LANES), jnp.float32)
    for a in range(ROWS // PITCH):
        for b in range(LANES // PITCH):
            flag = flags[b, a] if transposed else flags[a, b]
            here = (sub == a * (PITCH // DEPTH)) & (lane == b * PITCH)
            out = jnp.where(here & (flag == 1), cushion_pieces, out)
    return out


def coefficients(cap, warm, warm_t, flags, x_ref, y_ref, cap_t, x_rows, y_rows, y_edges, y_pad):
    cap_t[...] = cap[...].T
    for transposed, caps, warms, ref, rows in (
        (False, cap, warm, x_ref, x_rows),
        (True, cap_t, warm_t, y_ref, y_rows),
    ):
        admittance = yward_admittance if transposed else xward_admittance
        temps = load_lines(warms)
        edges = {(r, r + 1): wire(admittance, temps[r], temps[r + 1]) for r in range(DEPTH - 1)}
        across = wire(admittance, temps[DEPTH - 1], roll(temps[0], -1))
        pad = pads(flags, transposed)
        if transposed:
            store_regs(y_edges, [edges[(r, r + 1)] for r in range(DEPTH - 1)] + [across])
            y_pad[...] = pad
        ground = load_lines(caps)
        ground[0] = ground[0] + pad
        own, first, end = factor_local(ref, ground, edges, across)
        rows[...] = jnp.zeros((SUB, LANES), jnp.float32)
        rows[2:3, :] = first
        rows[3:4, :] = end
        rows[4:5, :] = own
        if not transposed:
            rows[5:6, :] = warms[0:1, :]
            rows[6:7, :] = warms[ROWS - 1 : ROWS, :]


def begin(
    v_t, warm_t, cap_t, load, inside, outside, y_edges, y_pad, y_rows, x_ref, x_rows,
    s_out, f_out, sent, y_rows_out, flat,
):
    sub = sublanes()
    place = lax.axis_index("gy")
    odd = lax.rem(place, 2) == 1
    low_v = jnp.where(odd, inside[0:1, :], outside[0:1, :])
    low_warm = jnp.where(odd, inside[1:2, :], outside[1:2, :])
    high_v = jnp.where(odd, outside[0:1, :], inside[0:1, :])
    high_warm = jnp.where(odd, outside[1:2, :], inside[1:2, :])
    low_edge = wire(yward_admittance, low_warm, warm_t[0:1, :])
    high_edge = wire(yward_admittance, warm_t[ROWS - 1 : ROWS, :], high_warm)
    low_edge = jnp.where(place > 0, low_edge, 0.0)
    high_edge = jnp.where(place < COUNT_Y - 1, high_edge, 0.0)
    y_rows_out[...] = y_rows[...]
    y_rows_out[5:6, :] = high_edge
    v = load_lines(v_t)
    cap = load_lines(cap_t)
    edges = load_regs(y_edges)
    before = jnp.where(sub == 0, spread(low_v), roll(v[DEPTH - 1], 1))
    before_edge = jnp.where(sub == 0, spread(low_edge), roll(edges[DEPTH - 1], 1))
    after = jnp.where(sub == SUB - 1, spread(high_v), roll(v[0], -1))
    edges[DEPTH - 1] = jnp.where(sub == SUB - 1, spread(high_edge), edges[DEPTH - 1])
    flow = before_edge * (before - v[0])
    out = []
    for r in range(DEPTH):
        onward = edges[r] * ((v[r + 1] if r + 1 < DEPTH else after) - v[r])
        own = cap[r] * v[r]
        if r == 0:
            own = own - y_pad[...] * v[r]
        out.append(own + (flow + onward))
        flow = -onward
    store_lines(flat, out)
    flat[...] = flat[...].T + load[0]
    s = load_lines(flat)
    store_regs(s_out, s)
    first, end = forward_local(x_ref, s)
    store_regs(f_out, s)
    sent[...] = x_rows[...]
    sent[0:1, :] = first
    sent[1:2, :] = end


def across_x(
    own, one, two, three, cap, load, step, s_in, f_in, x_ref, y_ref, x_join, s_out, f_out, joined, flat
):
    first, end = solve_x(x_join, joined)
    half = backward_local(x_ref, load_regs(f_in), first, end)
    caps, source = load_lines(cap), load_regs(s_in)
    loads = load_lines(load.at[step])
    store_lines(
        flat, [2.0 * caps[r] * half[r] - source[r] + loads[r] for r in range(DEPTH)]
    )
    flat[...] = flat[...].T
    s = load_lines(flat)
    if s_out is not None:
        store_regs(s_out, s)
    ends = forward_local(y_ref, s)
    store_regs(f_out, s)
    return ends


def first_x(
    own, one, two, three, cap, load, s_in, f_in, x_ref, y_ref, y_rows,
    x_join, s_out, f_out, sent, joined, flat,
):
    gather_x(joined, own, (one, two, three))
    factor_x(x_join, joined)
    first, end = across_x(
        own, one, two, three, cap, load, 0, s_in, f_in, x_ref, y_ref, x_join, s_out, f_out, joined, flat
    )
    sent[...] = y_rows[...]
    sent[0:1, :] = first
    sent[1:2, :] = end


def second_x(
    own, one, two, three, cap, load, s_in, f_in, x_ref, y_ref, x_join, f_out, sent, joined, flat
):
    gather_x(joined, own, (one, two, three))
    first, end = across_x(
        own, one, two, three, cap, load, 1, s_in, f_in, x_ref, y_ref, x_join, None, f_out, joined, flat
    )
    sent[0:1, :] = first
    sent[1:2, :] = end


def first_y(
    joined, cap_t, load, s_in, f_in, y_ref, x_ref, y_join, s_out, f_out, sent, found, flat
):
    factor_y(y_join, joined)
    first, end = solve_y(y_join, joined, SUB, found)
    drop = backward_local(y_ref, load_regs(f_in), first, end)
    caps, source = load_lines(cap_t), load_regs(s_in)
    store_lines(flat, [2.0 * caps[r] * drop[r] - source[r] for r in range(DEPTH)])
    flat[...] = flat[...].T + load[1]
    s = load_lines(flat)
    store_regs(s_out, s)
    first, end = forward_local(x_ref, s)
    store_regs(f_out, s)
    sent[0:1, :] = first
    sent[1:2, :] = end


def second_y(joined, f_in, y_ref, y_join, out, found, flat):
    first, end = solve_y(y_join, joined, 2, found)
    store_lines(flat, backward_local(y_ref, load_regs(f_in), first, end))
    out[...] = flat[...].T


def call(body, shapes, args, scratch=(), scalars=(), near=True):
    args = [
        x if n in scalars else pltpu.with_memory_space_constraint(x, pltpu.VMEM)
        for n, x in enumerate(args)
    ]
    made = pltpu.VMEM if near else jax.ShapeDtypeStruct
    specs = [
        pl.BlockSpec(memory_space=pltpu.SMEM if n in scalars else pltpu.VMEM)
        for n in range(len(args))
    ]
    return pl.pallas_call(
        body,
        out_shape=[made((rows, LANES), jnp.float32) for rows in shapes],
        in_specs=specs,
        out_specs=[pl.BlockSpec(memory_space=pltpu.VMEM)] * len(shapes),
        scratch_shapes=[pltpu.VMEM((rows, LANES), jnp.float32) for rows in scratch],
        name=body.__name__,
    )(*args)


def share_x(sent):
    return [
        lax.ppermute(sent, "gx", [(i, (i + by) % COUNT_X) for i in range(COUNT_X)])
        for by in range(1, COUNT_X)
    ]


def share_y(sent):
    rows = sent.shape[0]
    copies = jnp.broadcast_to(sent[None], (COUNT_Y, rows, LANES))
    return lax.all_to_all(copies, "gy", split_axis=0, concat_axis=0, tiled=True).reshape(
        COUNT_Y * rows, LANES
    )


def local(starting_sag, warmth_celsius_field, junction_charge_store, load_amperes, source_patch_bits):
    v, warm, cap, load = starting_sag, warmth_celsius_field, junction_charge_store, load_amperes
    v_t, warm_t, inside, outside = call(prepare, (ROWS, ROWS, 2, 2), (v, warm))
    inside = lax.ppermute(inside, "gy", [(i, i ^ 1) for i in range(COUNT_Y)])
    pairs = [(i, (i + 1) % COUNT_Y if i % 2 else (i - 1) % COUNT_Y) for i in range(COUNT_Y)]
    outside = lax.ppermute(outside, "gy", pairs)
    coefs = SUB * LOCAL_COEFS
    x_ref, y_ref, cap_t, x_rows, y_rows, y_edges, y_pad = call(
        coefficients,
        (coefs, coefs, ROWS, SUB, SUB, ROWS, SUB),
        (cap, warm, warm_t, source_patch_bits),
        scalars=(3,),
    )
    s, f, sent, y_rows = call(
        begin,
        (ROWS, ROWS, SUB, SUB),
        (v_t, warm_t, cap_t, load, inside, outside, y_edges, y_pad, y_rows, x_ref, x_rows),
        scratch=(ROWS,),
    )
    joined = COUNT_X * SUB
    x_join, s, f, sent = call(
        first_x,
        (SUB * X_COEFS, ROWS, ROWS, SUB),
        (sent, *share_x(sent), cap, load, s, f, x_ref, y_ref, y_rows),
        scratch=(joined, ROWS),
    )
    y_join, s, f, sent = call(
        first_y,
        (SUB * Y_COEFS, ROWS, ROWS, 2),
        (share_y(sent), cap_t, load, s, f, y_ref, x_ref),
        scratch=(2 * Y_DEPTH * SUB, ROWS),
    )
    f, sent = call(
        second_x,
        (ROWS, 2),
        (sent, *share_x(sent), cap, load, s, f, x_ref, y_ref, x_join),
        scratch=(joined, ROWS),
    )
    (drop,) = call(
        second_y,
        (ROWS,),
        (share_y(sent), f, y_ref, y_join),
        scratch=(2 * Y_DEPTH * SUB, ROWS),
        near=False,
    )
    return drop


def solution(mesh):
    return jax.shard_map(
        local,
        mesh=mesh,
        in_specs=(P("gx", "gy"), P("gx", "gy"), P("gx", "gy"), P(None, "gx", "gy"), P("gx", "gy")),
        out_specs=P("gx", "gy"),
        check_vma=False,
    )
```

```python
import jax
import jax.numpy as jnp
from jax import lax
from jax.experimental import pallas as pl
from jax.experimental.pallas import tpu as pltpu
from jax.sharding import PartitionSpec as P

PITCH = 32
xward_admittance = 1.0
yward_admittance = 0.5
warmth_scaling = 0.004
surrounding_warmth = 25.0
cushion_pieces = 1.0

SUB = 8
LANES = 128
ROWS = 128
DEPTH = ROWS // SUB
COUNT_X = 4
COUNT_Y = 32
Y_DEPTH = COUNT_Y // SUB

INNER = (
    [(m, m - 1, m + 1) for m in range(1, DEPTH - 2, 2)]
    + [(2, 0, 4), (6, 4, 8), (10, 8, 12), (14, 12, 15)]
    + [(4, 0, 8), (12, 8, 15), (8, 0, 15)]
)
SPANS = (1, 2, 4)
LOCAL_COEFS = 3 * (len(INNER) + 1 + len(SPANS))

def path_order(nodes):
    order = []
    while len(nodes) > 1:
        for at in range(1, len(nodes), 2):
            right = nodes[at + 1] if at + 1 < len(nodes) else None
            order.append((nodes[at], nodes[at - 1], right))
        nodes = nodes[::2]
    return order + [(nodes[0], None, None)]


X_ORDER = path_order(list(range(2 * COUNT_X)))
X_COEFS = 3 * len(X_ORDER)
Y_ORDER = [(1, 0, 2), (3, 2, 4), (5, 4, 6), (7, 6, 8), (2, 0, 4), (6, 4, 8), (4, 0, 8)]
Y_COEFS = 3 * (len(Y_ORDER) + len(SPANS)) + 1


def wire(admittance, warm_a, warm_b):
    return admittance / (1.0 + warmth_scaling * (0.5 * (warm_a + warm_b) - surrounding_warmth))


def sublanes():
    return lax.broadcasted_iota(jnp.int32, (SUB, LANES), 0)


def roll(x, by):
    return pltpu.roll(x, by % SUB, 0)


def spread(row):
    return jnp.broadcast_to(row, (SUB, LANES))


def load_lines(ref):
    return [ref[pl.ds(r, SUB, stride=DEPTH), :] for r in range(DEPTH)]


def store_lines(ref, values):
    for r in range(DEPTH):
        ref[pl.ds(r, SUB, stride=DEPTH), :] = values[r]


def load_regs(ref, count=DEPTH):
    return [ref[pl.ds(SUB * r, SUB), :] for r in range(count)]


def store_regs(ref, values):
    for r, value in enumerate(values):
        ref[pl.ds(SUB * r, SUB), :] = value


def coef(ref, k):
    return [ref[pl.ds(SUB * (3 * k + n), SUB), :] for n in range(3)]


def put_coef(ref, k, values):
    for n, value in enumerate(values):
        ref[pl.ds(SUB * (3 * k + n), SUB), :] = value


def factor_local(ref, ground, edges, across):
    sub = sublanes()
    edges = dict(edges)
    for k, (m, left, right) in enumerate(INNER):
        to_left, to_right = edges[(left, m)], edges[(m, right)]
        inverse = 1.0 / (to_left + to_right + ground[m])
        by_left, by_right = to_left * inverse, to_right * inverse
        ground[left] = ground[left] + by_left * ground[m]
        ground[right] = ground[right] + by_right * ground[m]
        edges[(left, right)] = to_left * by_right
        put_coef(ref, k, (inverse, by_left, by_right))
    own, first, last = edges[(0, DEPTH - 1)], ground[0], ground[DEPTH - 1]
    inside = sub < SUB - 1
    inverse = jnp.where(inside, 1.0 / (own + across + last), 0.0)
    by_left, by_right = own * inverse, across * inverse
    put_coef(ref, len(INNER), (inverse, by_left, by_right))
    edge = jnp.where(inside, own * by_right, own)
    end = roll(last, 1)
    first = first + by_left * last + roll(by_right * last, 1)
    for n, span in enumerate(SPANS):
        chosen = sub % (2 * span) == span
        to_left = roll(edge, span)
        inverse = jnp.where(chosen, 1.0 / (to_left + edge + first), 0.0)
        by_left, by_right = to_left * inverse, edge * inverse
        put_coef(ref, len(INNER) + 1 + n, (inverse, by_left, by_right))
        passed = roll(by_right * first, span)
        end = end + passed
        first = first + roll(by_left * first, -span) + jnp.where(sub == 0, 0.0, passed)
        edge = roll(to_left * by_right, -span)
    return edge[0:1], first[0:1], end[0:1]


def forward_local(ref, f):
    sub = sublanes()
    for k, (m, left, right) in enumerate(INNER):
        _, by_left, by_right = coef(ref, k)
        f[left] = f[left] + by_left * f[m]
        f[right] = f[right] + by_right * f[m]
    first, last = f[0], f[DEPTH - 1]
    _, by_left, by_right = coef(ref, len(INNER))
    end = roll(last, 1)
    first = first + by_left * last + roll(by_right * last, 1)
    for n, span in enumerate(SPANS):
        _, by_left, by_right = coef(ref, len(INNER) + 1 + n)
        passed = roll(by_right * first, span)
        end = end + passed
        first = first + roll(by_left * first, -span) + jnp.where(sub == 0, 0.0, passed)
    f[0] = first
    return first[0:1], end[0:1]


def backward_local(ref, f, first, end):
    sub = sublanes()
    x = jnp.where(sub == 0, first, 0.0)
    for n in range(len(SPANS) - 1, -1, -1):
        span = SPANS[n]
        inverse, by_left, by_right = coef(ref, len(INNER) + 1 + n)
        beyond = roll(jnp.where(sub == 0, end, x), -span)
        found = inverse * f[0] + by_left * roll(x, span) + by_right * beyond
        x = jnp.where(sub % (2 * span) == span, found, x)
    inverse, by_left, by_right = coef(ref, len(INNER))
    found = inverse * f[DEPTH - 1] + by_left * x + by_right * roll(x, -1)
    out = [None] * DEPTH
    out[0] = x
    out[DEPTH - 1] = jnp.where(sub == SUB - 1, end, found)
    for k in range(len(INNER) - 1, -1, -1):
        m, left, right = INNER[k]
        inverse, by_left, by_right = coef(ref, k)
        out[m] = inverse * f[m] + by_left * out[left] + by_right * out[right]
    return out


def put_rows(ref, rows):
    for n, row in enumerate(rows):
        ref[n : n + 1, :] = row


def gather_x(joined, own, others):
    place = lax.axis_index("gx")
    count = own.shape[0]
    joined[pl.ds(pl.multiple_of(place * SUB, SUB), count), :] = own[...]
    for n, other in enumerate(others):
        source = jnp.bitwise_xor(place, n + 1)
        joined[pl.ds(pl.multiple_of(source * SUB, SUB), count), :] = other[...]


def factor_x(ref, joined):
    def row(p, q):
        return spread(joined[SUB * p + q : SUB * p + q + 1, :])

    ground, edges = {}, {}
    for p in range(COUNT_X):
        ground[2 * p], ground[2 * p + 1] = row(p, 2), row(p, 3)
        edges[(2 * p, 2 * p + 1)] = row(p, 4)
        if p + 1 < COUNT_X:
            edges[(2 * p + 1, 2 * p + 2)] = wire(xward_admittance, row(p, 6), row(p + 1, 5))
    for k, (m, left, right) in enumerate(X_ORDER):
        total = ground[m]
        if left is not None:
            total = total + edges[(left, m)]
        if right is not None:
            total = total + edges[(m, right)]
        inverse = 1.0 / total
        by_left = edges[(left, m)] * inverse if left is not None else inverse
        by_right = edges[(m, right)] * inverse if right is not None else inverse
        if left is not None:
            ground[left] = ground[left] + by_left * ground[m]
        if right is not None:
            ground[right] = ground[right] + by_right * ground[m]
        if left is not None and right is not None:
            edges[(left, right)] = edges[(left, m)] * by_right
        put_coef(ref, k, (inverse, by_left, by_right))


def solve_x(ref, joined):
    f = [
        spread(joined[SUB * (n // 2) + n % 2 : SUB * (n // 2) + n % 2 + 1, :])
        for n in range(2 * COUNT_X)
    ]
    for k, (m, left, right) in enumerate(X_ORDER):
        _, by_left, by_right = coef(ref, k)
        if left is not None:
            f[left] = f[left] + by_left * f[m]
        if right is not None:
            f[right] = f[right] + by_right * f[m]
    x = [None] * len(f)
    for k in range(len(X_ORDER) - 1, -1, -1):
        m, left, right = X_ORDER[k]
        inverse, by_left, by_right = coef(ref, k)
        x[m] = inverse * f[m]
        if left is not None:
            x[m] = x[m] + by_left * x[left]
        if right is not None:
            x[m] = x[m] + by_right * x[right]
    place = lax.axis_index("gx")
    first, end = x[0], x[1]
    for p in range(1, COUNT_X):
        first = jnp.where(place == p, x[2 * p], first)
        end = jnp.where(place == p, x[2 * p + 1], end)
    return first, end


def factor_y(ref, joined):
    sub = sublanes()

    def part(r, q):
        return joined[pl.ds(SUB * r + q, SUB, stride=SUB * Y_DEPTH), :]

    ground, edges = {}, {}
    for r in range(Y_DEPTH):
        ground[2 * r], ground[2 * r + 1] = part(r, 2), part(r, 3)
        edges[(2 * r, 2 * r + 1)], edges[(2 * r + 1, 2 * r + 2)] = part(r, 4), part(r, 5)
    last = 2 * Y_DEPTH
    for k, (m, left, right) in enumerate(Y_ORDER):
        to_left, to_right = edges[(left, m)], edges[(m, right)]
        inverse = 1.0 / (to_left + to_right + ground[m])
        by_left, by_right = to_left * inverse, to_right * inverse
        put_coef(ref, k, (inverse, by_left, by_right))
        ground[left] = ground[left] + by_left * ground[m]
        passed = by_right * ground[m]
        if right == last:
            ground[0] = ground[0] + roll(passed, 1)
        else:
            ground[right] = ground[right] + passed
        edges[(left, right)] = to_left * by_right
    edge, first = edges[(0, last)], ground[0]
    for n, span in enumerate(SPANS):
        chosen = sub % (2 * span) == span
        to_left = roll(edge, span)
        inverse = jnp.where(chosen, 1.0 / (to_left + edge + first), 0.0)
        by_left, by_right = to_left * inverse, edge * inverse
        put_coef(ref, len(Y_ORDER) + n, (inverse, by_left, by_right))
        first = first + roll(by_left * first, -span) + roll(by_right * first, span)
        edge = roll(to_left * by_right, -span)
    ref[pl.ds(SUB * (Y_COEFS - 1), SUB), :] = jnp.where(sub == 0, 1.0 / first, 0.0)


def solve_y(ref, joined, stride, found):
    sub = sublanes()
    last = 2 * Y_DEPTH
    f = [
        joined[pl.ds(stride * (n // 2) + n % 2, SUB, stride=stride * Y_DEPTH), :]
        for n in range(last)
    ]
    for k, (m, left, right) in enumerate(Y_ORDER):
        _, by_left, by_right = coef(ref, k)
        f[left] = f[left] + by_left * f[m]
        if right == last:
            f[0] = f[0] + roll(by_right * f[m], 1)
        else:
            f[right] = f[right] + by_right * f[m]
    first = f[0]
    for n, span in enumerate(SPANS):
        _, by_left, by_right = coef(ref, len(Y_ORDER) + n)
        first = first + roll(by_left * first, -span) + roll(by_right * first, span)
    x0 = ref[pl.ds(SUB * (Y_COEFS - 1), SUB), :] * first
    for n in range(len(SPANS) - 1, -1, -1):
        span = SPANS[n]
        inverse, by_left, by_right = coef(ref, len(Y_ORDER) + n)
        value = inverse * first + by_left * roll(x0, span) + by_right * roll(x0, -span)
        x0 = jnp.where(sub % (2 * span) == span, value, x0)
    x = [x0] + [None] * (last - 1) + [roll(x0, -1)]
    for k in range(len(Y_ORDER) - 1, -1, -1):
        m, left, right = Y_ORDER[k]
        inverse, by_left, by_right = coef(ref, k)
        x[m] = inverse * f[m] + by_left * x[left] + by_right * x[right]
    store_regs(found, x[:last])
    place = lax.axis_index("gy")
    at = lax.rem(place, Y_DEPTH) * (2 * SUB) + lax.div(place, Y_DEPTH)
    return spread(found[pl.ds(at, 1), :]), spread(found[pl.ds(at + SUB, 1), :])


def put_rim(ref, v_t, warm_t, low):
    for n, block in enumerate((v_t, warm_t)):
        ref[n : n + 1, :] = jnp.where(low, block[0:1, :], block[ROWS - 1 : ROWS, :])


def prepare(v, warm, v_t, warm_t, outside):
    v_t[...] = v[...].T
    warm_t[...] = warm[...].T
    put_rim(outside, v_t, warm_t, lax.rem(lax.axis_index("gy"), 2) == 0)


def pads(flags, transposed):
    sub = sublanes()
    lane = lax.broadcasted_iota(jnp.int32, (SUB, LANES), 1)
    out = jnp.zeros((SUB, LANES), jnp.float32)
    for a in range(ROWS // PITCH):
        for b in range(LANES // PITCH):
            row, col = (b, a) if transposed else (a, b)
            flag = spread(flags[row : row + 1, col : col + 1])
            here = (sub == a * (PITCH // DEPTH)) & (lane == b * PITCH)
            out = jnp.where(here & (flag == 1), cushion_pieces, out)
    return out


def put_ends(rows, own, first, end):
    rows[...] = jnp.zeros((SUB, LANES), jnp.float32)
    rows[2:3, :] = first
    rows[3:4, :] = end
    rows[4:5, :] = own


def factor_lines_x(
    cap, warm, v_t, warm_t, flags, x_ref, x_rows, cap_t, y_edges, y_pad, inside
):
    put_rim(inside, v_t, warm_t, lax.rem(lax.axis_index("gy"), 2) == 1)
    cap_t[...] = cap[...].T
    temps = load_lines(warm_t)
    store_regs(
        y_edges,
        [wire(yward_admittance, temps[r], temps[r + 1]) for r in range(DEPTH - 1)]
        + [wire(yward_admittance, temps[DEPTH - 1], roll(temps[0], -1))],
    )
    y_pad[...] = pads(flags, True)
    temps = load_lines(warm)
    edges = {
        (r, r + 1): wire(xward_admittance, temps[r], temps[r + 1]) for r in range(DEPTH - 1)
    }
    across = wire(xward_admittance, temps[DEPTH - 1], roll(temps[0], -1))
    ground = load_lines(cap)
    ground[0] = ground[0] + pads(flags, False)
    put_ends(x_rows, *factor_local(x_ref, ground, edges, across))
    x_rows[5:6, :] = warm[0:1, :]
    x_rows[6:7, :] = warm[ROWS - 1 : ROWS, :]


def factor_lines_y(cap_t, y_edges, y_pad, y_ref, y_rows):
    edges = load_regs(y_edges)
    ground = load_lines(cap_t)
    ground[0] = ground[0] + y_pad[...]
    inner = {(r, r + 1): edges[r] for r in range(DEPTH - 1)}
    put_ends(y_rows, *factor_local(y_ref, ground, inner, edges[DEPTH - 1]))


def begin(
    v_t, warm_t, cap_t, load, inside, outside, y_edges, y_pad, x_ref, x_rows,
    s_out, f_out, sent, y_high, flat,
):
    sub = sublanes()
    place = lax.axis_index("gy")
    odd = lax.rem(place, 2) == 1
    low_v = jnp.where(odd, inside[0:1, :], outside[0:1, :])
    low_warm = jnp.where(odd, inside[1:2, :], outside[1:2, :])
    high_v = jnp.where(odd, outside[0:1, :], inside[0:1, :])
    high_warm = jnp.where(odd, outside[1:2, :], inside[1:2, :])
    low_edge = wire(yward_admittance, low_warm, warm_t[0:1, :])
    high_edge = wire(yward_admittance, warm_t[ROWS - 1 : ROWS, :], high_warm)
    low_edge = jnp.where(place > 0, low_edge, 0.0)
    high_edge = jnp.where(place < COUNT_Y - 1, high_edge, 0.0)
    y_high[...] = high_edge
    v = load_lines(v_t)
    cap = load_lines(cap_t)
    edges = load_regs(y_edges)
    before = jnp.where(sub == 0, spread(low_v), roll(v[DEPTH - 1], 1))
    before_edge = jnp.where(sub == 0, spread(low_edge), roll(edges[DEPTH - 1], 1))
    after = jnp.where(sub == SUB - 1, spread(high_v), roll(v[0], -1))
    edges[DEPTH - 1] = jnp.where(sub == SUB - 1, spread(high_edge), edges[DEPTH - 1])
    flow = before_edge * (before - v[0])
    out = []
    for r in range(DEPTH):
        onward = edges[r] * ((v[r + 1] if r + 1 < DEPTH else after) - v[r])
        own = cap[r] * v[r]
        if r == 0:
            own = own - y_pad[...] * v[r]
        out.append(own + (flow + onward))
        flow = -onward
    store_lines(flat, out)
    flat[...] = flat[...].T + load[0]
    s = load_lines(flat)
    store_regs(s_out, s)
    first, end = forward_local(x_ref, s)
    store_regs(f_out, s)
    sent[...] = x_rows[...]
    sent[0:1, :] = first
    sent[1:2, :] = end


def across_x(
    own, one, two, three, cap, load, step, s_in, f_in, x_ref, y_ref, x_join, s_out, f_out, joined, flat
):
    first, end = solve_x(x_join, joined)
    half = backward_local(x_ref, load_regs(f_in), first, end)
    caps, source = load_lines(cap), load_regs(s_in)
    loads = load_lines(load.at[step])
    store_lines(
        flat, [2.0 * caps[r] * half[r] - source[r] + loads[r] for r in range(DEPTH)]
    )
    flat[...] = flat[...].T
    s = load_lines(flat)
    if s_out is not None:
        store_regs(s_out, s)
    ends = forward_local(y_ref, s)
    store_regs(f_out, s)
    return ends


def first_x(
    own, one, two, three, cap, load, s_in, f_in, x_ref, y_ref, y_rows, y_high,
    x_join, s_out, f_out, sent, joined, flat,
):
    gather_x(joined, own, (one, two, three))
    factor_x(x_join, joined)
    first, end = across_x(
        own, one, two, three, cap, load, 0, s_in, f_in, x_ref, y_ref, x_join, s_out, f_out, joined, flat
    )
    sent[...] = y_rows[...]
    sent[0:1, :] = first
    sent[1:2, :] = end
    sent[5:6, :] = y_high[...]


def second_x(
    own, one, two, three, cap, load, s_in, f_in, x_ref, y_ref, x_join, f_out, sent, joined, flat
):
    gather_x(joined, own, (one, two, three))
    first, end = across_x(
        own, one, two, three, cap, load, 1, s_in, f_in, x_ref, y_ref, x_join, None, f_out, joined, flat
    )
    sent[0:1, :] = first
    sent[1:2, :] = end


def first_y(
    joined, cap_t, load, s_in, f_in, y_ref, x_ref, y_join, s_out, f_out, sent, found, flat
):
    factor_y(y_join, joined)
    first, end = solve_y(y_join, joined, SUB, found)
    drop = backward_local(y_ref, load_regs(f_in), first, end)
    caps, source = load_lines(cap_t), load_regs(s_in)
    store_lines(flat, [2.0 * caps[r] * drop[r] - source[r] for r in range(DEPTH)])
    flat[...] = flat[...].T + load[1]
    s = load_lines(flat)
    store_regs(s_out, s)
    first, end = forward_local(x_ref, s)
    store_regs(f_out, s)
    sent[0:1, :] = first
    sent[1:2, :] = end


def second_y(joined, f_in, y_ref, y_join, out, found, flat):
    first, end = solve_y(y_join, joined, 2, found)
    store_lines(flat, backward_local(y_ref, load_regs(f_in), first, end))
    out[...] = flat[...].T


def call(body, shapes, args, scratch=(), fetched=True, near=True):
    if fetched:
        args = [pltpu.with_memory_space_constraint(x, pltpu.VMEM) for x in args]
    made = pltpu.VMEM if near else jax.ShapeDtypeStruct
    return pl.pallas_call(
        body,
        out_shape=[made((rows, LANES), jnp.float32) for rows in shapes],
        in_specs=[pl.BlockSpec(memory_space=pltpu.VMEM)] * len(args),
        out_specs=[pl.BlockSpec(memory_space=pltpu.VMEM)] * len(shapes),
        scratch_shapes=[pltpu.VMEM((rows, LANES), jnp.float32) for rows in scratch],
        name=body.__name__,
    )(*args)


def share_x(sent):
    return [
        lax.ppermute(sent, "gx", [(i, i ^ by) for i in range(COUNT_X)])
        for by in range(1, COUNT_X)
    ]


def share_y(sent):
    rows = sent.shape[0]
    copies = jnp.broadcast_to(sent[None], (COUNT_Y, rows, LANES))
    return lax.all_to_all(copies, "gy", split_axis=0, concat_axis=0, tiled=True).reshape(
        COUNT_Y * rows, LANES
    )


def outside_pairs():
    pairs = []
    for x in range(COUNT_X):
        for y in range(COUNT_Y):
            if y in (0, COUNT_Y - 1):
                to = ((x ^ 1), y)
            else:
                to = (x, y + 1 if y % 2 else y - 1)
            pairs.append((x * COUNT_Y + y, to[0] * COUNT_Y + to[1]))
    return pairs


def local(starting_sag, warmth_celsius_field, junction_charge_store, load_amperes, source_patch_bits):
    v, warm, cap, load = starting_sag, warmth_celsius_field, junction_charge_store, load_amperes
    v_t, warm_t, outside = call(prepare, (ROWS, ROWS, 2), (v, warm), fetched=False)
    outside = lax.ppermute(outside, ("gx", "gy"), outside_pairs())
    coefs = SUB * LOCAL_COEFS
    x_ref, x_rows, cap_t, y_edges, y_pad, inside = call(
        factor_lines_x,
        (coefs, SUB, ROWS, ROWS, SUB, 2),
        (cap, warm, v_t, warm_t, source_patch_bits),
    )
    inside = lax.ppermute(inside, "gy", [(i, i ^ 1) for i in range(COUNT_Y)])
    y_ref, y_rows = call(factor_lines_y, (coefs, SUB), (cap_t, y_edges, y_pad))
    s, f, sent, y_high = call(
        begin,
        (ROWS, ROWS, SUB, 1),
        (v_t, warm_t, cap_t, load, inside, outside, y_edges, y_pad, x_ref, x_rows),
        scratch=(ROWS,),
    )
    joined = COUNT_X * SUB
    x_join, s, f, sent = call(
        first_x,
        (SUB * X_COEFS, ROWS, ROWS, SUB),
        (sent, *share_x(sent), cap, load, s, f, x_ref, y_ref, y_rows, y_high),
        scratch=(joined, ROWS),
    )
    y_join, s, f, sent = call(
        first_y,
        (SUB * Y_COEFS, ROWS, ROWS, 2),
        (share_y(sent), cap_t, load, s, f, y_ref, x_ref),
        scratch=(2 * Y_DEPTH * SUB, ROWS),
    )
    f, sent = call(
        second_x,
        (ROWS, 2),
        (sent, *share_x(sent), cap, load, s, f, x_ref, y_ref, x_join),
        scratch=(joined, ROWS),
    )
    (drop,) = call(
        second_y,
        (ROWS,),
        (share_y(sent), f, y_ref, y_join),
        scratch=(2 * Y_DEPTH * SUB, ROWS),
        near=False,
    )
    return drop


def solution(mesh):
    return jax.shard_map(
        local,
        mesh=mesh,
        in_specs=(P("gx", "gy"), P("gx", "gy"), P("gx", "gy"), P(None, "gx", "gy"), P("gx", "gy")),
        out_specs=P("gx", "gy"),
        check_vma=False,
    )
```

```python
import jax
import jax.numpy as jnp
from jax import lax
from jax.experimental import pallas as pl
from jax.experimental.pallas import tpu as pltpu
from jax.sharding import PartitionSpec as P

PITCH = 32
xward_admittance = 1.0
yward_admittance = 0.5
warmth_scaling = 0.004
surrounding_warmth = 25.0
cushion_pieces = 1.0

SUB = 8
LANES = 128
ROWS = 128
DEPTH = ROWS // SUB
COUNT_X = 4
COUNT_Y = 32
Y_DEPTH = COUNT_Y // SUB

INNER = (
    [(m, m - 1, m + 1) for m in range(1, DEPTH - 2, 2)]
    + [(2, 0, 4), (6, 4, 8), (10, 8, 12), (14, 12, 15)]
    + [(4, 0, 8), (12, 8, 15), (8, 0, 15)]
)
SPANS = (1, 2, 4)
X_TURNS = (1, 3, 2)
LOCAL_COEFS = 3 * (len(INNER) + 1 + len(SPANS))

def path_order(nodes):
    order = []
    while len(nodes) > 1:
        for at in range(1, len(nodes), 2):
            right = nodes[at + 1] if at + 1 < len(nodes) else None
            order.append((nodes[at], nodes[at - 1], right))
        nodes = nodes[::2]
    return order + [(nodes[0], None, None)]


X_ORDER = path_order(list(range(2 * COUNT_X)))
X_COEFS = 3 * len(X_ORDER)
Y_ORDER = [(1, 0, 2), (3, 2, 4), (5, 4, 6), (7, 6, 8), (2, 0, 4), (6, 4, 8), (4, 0, 8)]
Y_COEFS = 3 * (len(Y_ORDER) + len(SPANS)) + 1


def wire(admittance, warm_a, warm_b):
    return admittance / (1.0 + warmth_scaling * (0.5 * (warm_a + warm_b) - surrounding_warmth))


def sublanes():
    return lax.broadcasted_iota(jnp.int32, (SUB, LANES), 0)


def roll(x, by):
    return pltpu.roll(x, by % SUB, 0)


def spread(row):
    return jnp.broadcast_to(row, (SUB, LANES))


def load_lines(ref):
    return [ref[pl.ds(r, SUB, stride=DEPTH), :] for r in range(DEPTH)]


def store_lines(ref, values):
    for r in range(DEPTH):
        ref[pl.ds(r, SUB, stride=DEPTH), :] = values[r]


def load_regs(ref, count=DEPTH):
    return [ref[pl.ds(SUB * r, SUB), :] for r in range(count)]


def store_regs(ref, values):
    for r, value in enumerate(values):
        ref[pl.ds(SUB * r, SUB), :] = value


def coef(ref, k):
    return [ref[pl.ds(SUB * (3 * k + n), SUB), :] for n in range(3)]


def put_coef(ref, k, values):
    for n, value in enumerate(values):
        ref[pl.ds(SUB * (3 * k + n), SUB), :] = value


def factor_local(ref, ground, edges, across):
    sub = sublanes()
    edges = dict(edges)
    for k, (m, left, right) in enumerate(INNER):
        to_left, to_right = edges[(left, m)], edges[(m, right)]
        inverse = 1.0 / (to_left + to_right + ground[m])
        by_left, by_right = to_left * inverse, to_right * inverse
        ground[left] = ground[left] + by_left * ground[m]
        ground[right] = ground[right] + by_right * ground[m]
        edges[(left, right)] = to_left * by_right
        put_coef(ref, k, (inverse, by_left, by_right))
    own, first, last = edges[(0, DEPTH - 1)], ground[0], ground[DEPTH - 1]
    inside = sub < SUB - 1
    inverse = jnp.where(inside, 1.0 / (own + across + last), 0.0)
    by_left, by_right = own * inverse, across * inverse
    put_coef(ref, len(INNER), (inverse, by_left, by_right))
    edge = jnp.where(inside, own * by_right, own)
    end = roll(last, 1)
    first = first + by_left * last + roll(by_right * last, 1)
    for n, span in enumerate(SPANS):
        chosen = sub % (2 * span) == span
        to_left = roll(edge, span)
        inverse = jnp.where(chosen, 1.0 / (to_left + edge + first), 0.0)
        by_left, by_right = to_left * inverse, edge * inverse
        put_coef(ref, len(INNER) + 1 + n, (inverse, by_left, by_right))
        passed = roll(by_right * first, span)
        end = end + passed
        first = first + roll(by_left * first, -span) + jnp.where(sub == 0, 0.0, passed)
        edge = roll(to_left * by_right, -span)
    return edge[0:1], first[0:1], end[0:1]


def forward_local(ref, f):
    sub = sublanes()
    for k, (m, left, right) in enumerate(INNER):
        _, by_left, by_right = coef(ref, k)
        f[left] = f[left] + by_left * f[m]
        f[right] = f[right] + by_right * f[m]
    first, last = f[0], f[DEPTH - 1]
    _, by_left, by_right = coef(ref, len(INNER))
    end = roll(last, 1)
    first = first + by_left * last + roll(by_right * last, 1)
    for n, span in enumerate(SPANS):
        _, by_left, by_right = coef(ref, len(INNER) + 1 + n)
        passed = roll(by_right * first, span)
        end = end + passed
        first = first + roll(by_left * first, -span) + jnp.where(sub == 0, 0.0, passed)
    f[0] = first
    return first[0:1], end[0:1]


def backward_local(ref, f, first, end):
    sub = sublanes()
    x = jnp.where(sub == 0, first, 0.0)
    for n in range(len(SPANS) - 1, -1, -1):
        span = SPANS[n]
        inverse, by_left, by_right = coef(ref, len(INNER) + 1 + n)
        beyond = roll(jnp.where(sub == 0, end, x), -span)
        found = inverse * f[0] + by_left * roll(x, span) + by_right * beyond
        x = jnp.where(sub % (2 * span) == span, found, x)
    inverse, by_left, by_right = coef(ref, len(INNER))
    found = inverse * f[DEPTH - 1] + by_left * x + by_right * roll(x, -1)
    out = [None] * DEPTH
    out[0] = x
    out[DEPTH - 1] = jnp.where(sub == SUB - 1, end, found)
    for k in range(len(INNER) - 1, -1, -1):
        m, left, right = INNER[k]
        inverse, by_left, by_right = coef(ref, k)
        out[m] = inverse * f[m] + by_left * out[left] + by_right * out[right]
    return out


def put_rows(ref, rows):
    for n, row in enumerate(rows):
        ref[n : n + 1, :] = row


def gather_x(joined, own, others):
    place = lax.axis_index("gx")
    count = own.shape[0]
    joined[pl.ds(pl.multiple_of(place * SUB, SUB), count), :] = own[...]
    for n, other in enumerate(others):
        source = jnp.bitwise_xor(place, X_TURNS[n])
        joined[pl.ds(pl.multiple_of(source * SUB, SUB), count), :] = other[...]


def factor_x(ref, joined):
    def row(p, q):
        return spread(joined[SUB * p + q : SUB * p + q + 1, :])

    ground, edges = {}, {}
    for p in range(COUNT_X):
        ground[2 * p], ground[2 * p + 1] = row(p, 2), row(p, 3)
        edges[(2 * p, 2 * p + 1)] = row(p, 4)
        if p + 1 < COUNT_X:
            edges[(2 * p + 1, 2 * p + 2)] = wire(xward_admittance, row(p, 6), row(p + 1, 5))
    for k, (m, left, right) in enumerate(X_ORDER):
        total = ground[m]
        if left is not None:
            total = total + edges[(left, m)]
        if right is not None:
            total = total + edges[(m, right)]
        inverse = 1.0 / total
        by_left = edges[(left, m)] * inverse if left is not None else inverse
        by_right = edges[(m, right)] * inverse if right is not None else inverse
        if left is not None:
            ground[left] = ground[left] + by_left * ground[m]
        if right is not None:
            ground[right] = ground[right] + by_right * ground[m]
        if left is not None and right is not None:
            edges[(left, right)] = edges[(left, m)] * by_right
        put_coef(ref, k, (inverse, by_left, by_right))


def solve_x(ref, joined):
    f = [
        spread(joined[SUB * (n // 2) + n % 2 : SUB * (n // 2) + n % 2 + 1, :])
        for n in range(2 * COUNT_X)
    ]
    for k, (m, left, right) in enumerate(X_ORDER):
        _, by_left, by_right = coef(ref, k)
        if left is not None:
            f[left] = f[left] + by_left * f[m]
        if right is not None:
            f[right] = f[right] + by_right * f[m]
    x = [None] * len(f)
    for k in range(len(X_ORDER) - 1, -1, -1):
        m, left, right = X_ORDER[k]
        inverse, by_left, by_right = coef(ref, k)
        x[m] = inverse * f[m]
        if left is not None:
            x[m] = x[m] + by_left * x[left]
        if right is not None:
            x[m] = x[m] + by_right * x[right]
    place = lax.axis_index("gx")
    first, end = x[0], x[1]
    for p in range(1, COUNT_X):
        first = jnp.where(place == p, x[2 * p], first)
        end = jnp.where(place == p, x[2 * p + 1], end)
    return first, end


def factor_y(ref, joined):
    sub = sublanes()

    def part(r, q):
        return joined[pl.ds(SUB * r + q, SUB, stride=SUB * Y_DEPTH), :]

    ground, edges = {}, {}
    for r in range(Y_DEPTH):
        ground[2 * r], ground[2 * r + 1] = part(r, 2), part(r, 3)
        edges[(2 * r, 2 * r + 1)], edges[(2 * r + 1, 2 * r + 2)] = part(r, 4), part(r, 5)
    last = 2 * Y_DEPTH
    for k, (m, left, right) in enumerate(Y_ORDER):
        to_left, to_right = edges[(left, m)], edges[(m, right)]
        inverse = 1.0 / (to_left + to_right + ground[m])
        by_left, by_right = to_left * inverse, to_right * inverse
        put_coef(ref, k, (inverse, by_left, by_right))
        ground[left] = ground[left] + by_left * ground[m]
        passed = by_right * ground[m]
        if right == last:
            ground[0] = ground[0] + roll(passed, 1)
        else:
            ground[right] = ground[right] + passed
        edges[(left, right)] = to_left * by_right
    edge, first = edges[(0, last)], ground[0]
    for n, span in enumerate(SPANS):
        chosen = sub % (2 * span) == span
        to_left = roll(edge, span)
        inverse = jnp.where(chosen, 1.0 / (to_left + edge + first), 0.0)
        by_left, by_right = to_left * inverse, edge * inverse
        put_coef(ref, len(Y_ORDER) + n, (inverse, by_left, by_right))
        first = first + roll(by_left * first, -span) + roll(by_right * first, span)
        edge = roll(to_left * by_right, -span)
    ref[pl.ds(SUB * (Y_COEFS - 1), SUB), :] = jnp.where(sub == 0, 1.0 / first, 0.0)


def solve_y(ref, joined, stride, found):
    sub = sublanes()
    last = 2 * Y_DEPTH
    f = [
        joined[pl.ds(stride * (n // 2) + n % 2, SUB, stride=stride * Y_DEPTH), :]
        for n in range(last)
    ]
    for k, (m, left, right) in enumerate(Y_ORDER):
        _, by_left, by_right = coef(ref, k)
        f[left] = f[left] + by_left * f[m]
        if right == last:
            f[0] = f[0] + roll(by_right * f[m], 1)
        else:
            f[right] = f[right] + by_right * f[m]
    first = f[0]
    for n, span in enumerate(SPANS):
        _, by_left, by_right = coef(ref, len(Y_ORDER) + n)
        first = first + roll(by_left * first, -span) + roll(by_right * first, span)
    x0 = ref[pl.ds(SUB * (Y_COEFS - 1), SUB), :] * first
    for n in range(len(SPANS) - 1, -1, -1):
        span = SPANS[n]
        inverse, by_left, by_right = coef(ref, len(Y_ORDER) + n)
        value = inverse * first + by_left * roll(x0, span) + by_right * roll(x0, -span)
        x0 = jnp.where(sub % (2 * span) == span, value, x0)
    x = [x0] + [None] * (last - 1) + [roll(x0, -1)]
    for k in range(len(Y_ORDER) - 1, -1, -1):
        m, left, right = Y_ORDER[k]
        inverse, by_left, by_right = coef(ref, k)
        x[m] = inverse * f[m] + by_left * x[left] + by_right * x[right]
    store_regs(found, x[:last])
    place = lax.axis_index("gy")
    at = lax.rem(place, Y_DEPTH) * (2 * SUB) + lax.div(place, Y_DEPTH)
    return spread(found[pl.ds(at, 1), :]), spread(found[pl.ds(at + SUB, 1), :])


def put_rim(ref, v_t, warm_t, low):
    for n, block in enumerate((v_t, warm_t)):
        ref[n : n + 1, :] = jnp.where(low, block[0:1, :], block[ROWS - 1 : ROWS, :])


def prepare(v, warm, v_t, warm_t, outside):
    v_t[...] = v[...].T
    warm_t[...] = warm[...].T
    put_rim(outside, v_t, warm_t, lax.rem(lax.axis_index("gy"), 2) == 0)


def pads(flags, transposed):
    sub = sublanes()
    lane = lax.broadcasted_iota(jnp.int32, (SUB, LANES), 1)
    out = jnp.zeros((SUB, LANES), jnp.float32)
    for a in range(ROWS // PITCH):
        for b in range(LANES // PITCH):
            row, col = (b, a) if transposed else (a, b)
            flag = spread(flags[row : row + 1, col : col + 1])
            here = (sub == a * (PITCH // DEPTH)) & (lane == b * PITCH)
            out = jnp.where(here & (flag == 1), cushion_pieces, out)
    return out


def put_ends(rows, own, first, end):
    rows[...] = jnp.zeros((SUB, LANES), jnp.float32)
    rows[2:3, :] = first
    rows[3:4, :] = end
    rows[4:5, :] = own


def factor_lines_x(
    cap, warm, v_t, warm_t, flags, x_ref, x_rows, cap_t, y_edges, y_pad, inside
):
    put_rim(inside, v_t, warm_t, lax.rem(lax.axis_index("gy"), 2) == 1)
    cap_t[...] = cap[...].T
    temps = load_lines(warm_t)
    store_regs(
        y_edges,
        [wire(yward_admittance, temps[r], temps[r + 1]) for r in range(DEPTH - 1)]
        + [wire(yward_admittance, temps[DEPTH - 1], roll(temps[0], -1))],
    )
    y_pad[...] = pads(flags, True)
    temps = load_lines(warm)
    edges = {
        (r, r + 1): wire(xward_admittance, temps[r], temps[r + 1]) for r in range(DEPTH - 1)
    }
    across = wire(xward_admittance, temps[DEPTH - 1], roll(temps[0], -1))
    ground = load_lines(cap)
    ground[0] = ground[0] + pads(flags, False)
    put_ends(x_rows, *factor_local(x_ref, ground, edges, across))
    x_rows[5:6, :] = warm[0:1, :]
    x_rows[6:7, :] = warm[ROWS - 1 : ROWS, :]


def factor_lines_y(cap_t, y_edges, y_pad, y_ref, y_rows):
    edges = load_regs(y_edges)
    ground = load_lines(cap_t)
    ground[0] = ground[0] + y_pad[...]
    inner = {(r, r + 1): edges[r] for r in range(DEPTH - 1)}
    put_ends(y_rows, *factor_local(y_ref, ground, inner, edges[DEPTH - 1]))


def begin(
    v_t, warm_t, cap_t, load, inside, outside, y_edges, y_pad, x_ref, x_rows,
    s_out, f_out, sent, y_high, flat,
):
    sub = sublanes()
    place = lax.axis_index("gy")
    odd = lax.rem(place, 2) == 1
    low_v = jnp.where(odd, inside[0:1, :], outside[0:1, :])
    low_warm = jnp.where(odd, inside[1:2, :], outside[1:2, :])
    high_v = jnp.where(odd, outside[0:1, :], inside[0:1, :])
    high_warm = jnp.where(odd, outside[1:2, :], inside[1:2, :])
    low_edge = wire(yward_admittance, low_warm, warm_t[0:1, :])
    high_edge = wire(yward_admittance, warm_t[ROWS - 1 : ROWS, :], high_warm)
    low_edge = jnp.where(place > 0, low_edge, 0.0)
    high_edge = jnp.where(place < COUNT_Y - 1, high_edge, 0.0)
    y_high[...] = high_edge
    v = load_lines(v_t)
    cap = load_lines(cap_t)
    edges = load_regs(y_edges)
    before = jnp.where(sub == 0, spread(low_v), roll(v[DEPTH - 1], 1))
    before_edge = jnp.where(sub == 0, spread(low_edge), roll(edges[DEPTH - 1], 1))
    after = jnp.where(sub == SUB - 1, spread(high_v), roll(v[0], -1))
    edges[DEPTH - 1] = jnp.where(sub == SUB - 1, spread(high_edge), edges[DEPTH - 1])
    flow = before_edge * (before - v[0])
    out = []
    for r in range(DEPTH):
        onward = edges[r] * ((v[r + 1] if r + 1 < DEPTH else after) - v[r])
        own = cap[r] * v[r]
        if r == 0:
            own = own - y_pad[...] * v[r]
        out.append(own + (flow + onward))
        flow = -onward
    store_lines(flat, out)
    flat[...] = flat[...].T + load[0]
    s = load_lines(flat)
    store_regs(s_out, s)
    first, end = forward_local(x_ref, s)
    store_regs(f_out, s)
    sent[...] = x_rows[...]
    sent[0:1, :] = first
    sent[1:2, :] = end


def across_x(
    own, one, two, three, cap, load, step, s_in, f_in, x_ref, y_ref, x_join, s_out, f_out, joined, flat
):
    first, end = solve_x(x_join, joined)
    half = backward_local(x_ref, load_regs(f_in), first, end)
    caps, source = load_lines(cap), load_regs(s_in)
    loads = load_lines(load.at[step])
    store_lines(
        flat, [2.0 * caps[r] * half[r] - source[r] + loads[r] for r in range(DEPTH)]
    )
    flat[...] = flat[...].T
    s = load_lines(flat)
    if s_out is not None:
        store_regs(s_out, s)
    ends = forward_local(y_ref, s)
    store_regs(f_out, s)
    return ends


def first_x(
    own, one, two, three, cap, load, s_in, f_in, x_ref, y_ref, y_rows, y_high,
    x_join, s_out, f_out, sent, joined, flat,
):
    gather_x(joined, own, (one, two, three))
    factor_x(x_join, joined)
    first, end = across_x(
        own, one, two, three, cap, load, 0, s_in, f_in, x_ref, y_ref, x_join, s_out, f_out, joined, flat
    )
    sent[...] = y_rows[...]
    sent[0:1, :] = first
    sent[1:2, :] = end
    sent[5:6, :] = y_high[...]


def second_x(
    own, one, two, three, cap, load, s_in, f_in, x_ref, y_ref, x_join, f_out, sent, joined, flat
):
    gather_x(joined, own, (one, two, three))
    first, end = across_x(
        own, one, two, three, cap, load, 1, s_in, f_in, x_ref, y_ref, x_join, None, f_out, joined, flat
    )
    sent[0:1, :] = first
    sent[1:2, :] = end


def first_y(
    joined, cap_t, load, s_in, f_in, y_ref, x_ref, y_join, s_out, f_out, sent, found, flat
):
    factor_y(y_join, joined)
    first, end = solve_y(y_join, joined, SUB, found)
    drop = backward_local(y_ref, load_regs(f_in), first, end)
    caps, source = load_lines(cap_t), load_regs(s_in)
    store_lines(flat, [2.0 * caps[r] * drop[r] - source[r] for r in range(DEPTH)])
    flat[...] = flat[...].T + load[1]
    s = load_lines(flat)
    store_regs(s_out, s)
    first, end = forward_local(x_ref, s)
    store_regs(f_out, s)
    sent[0:1, :] = first
    sent[1:2, :] = end


def second_y(joined, f_in, y_ref, y_join, out, found, flat):
    first, end = solve_y(y_join, joined, 2, found)
    store_lines(flat, backward_local(y_ref, load_regs(f_in), first, end))
    out[...] = flat[...].T


def call(body, shapes, args, scratch=(), fetched=True, near=True):
    if fetched:
        args = [pltpu.with_memory_space_constraint(x, pltpu.VMEM) for x in args]
    made = pltpu.VMEM if near else jax.ShapeDtypeStruct
    return pl.pallas_call(
        body,
        out_shape=[made((rows, LANES), jnp.float32) for rows in shapes],
        in_specs=[pl.BlockSpec(memory_space=pltpu.VMEM)] * len(args),
        out_specs=[pl.BlockSpec(memory_space=pltpu.VMEM)] * len(shapes),
        scratch_shapes=[pltpu.VMEM((rows, LANES), jnp.float32) for rows in scratch],
        name=body.__name__,
    )(*args)


def share_x(sent):
    return [
        lax.ppermute(sent, "gx", [(i, i ^ by) for i in range(COUNT_X)])
        for by in X_TURNS
    ]


def share_y(sent):
    rows = sent.shape[0]
    copies = jnp.broadcast_to(sent[None], (COUNT_Y, rows, LANES))
    return lax.all_to_all(copies, "gy", split_axis=0, concat_axis=0, tiled=True).reshape(
        COUNT_Y * rows, LANES
    )


def outside_pairs():
    pairs = []
    for x in range(COUNT_X):
        for y in range(COUNT_Y):
            if y in (0, COUNT_Y - 1):
                to = ((x ^ 1), y)
            else:
                to = (x, y + 1 if y % 2 else y - 1)
            pairs.append((x * COUNT_Y + y, to[0] * COUNT_Y + to[1]))
    return pairs


def local(starting_sag, warmth_celsius_field, junction_charge_store, load_amperes, source_patch_bits):
    v, warm, cap, load = starting_sag, warmth_celsius_field, junction_charge_store, load_amperes
    v_t, warm_t, outside = call(prepare, (ROWS, ROWS, 2), (v, warm), fetched=False)
    outside = lax.ppermute(outside, ("gx", "gy"), outside_pairs())
    coefs = SUB * LOCAL_COEFS
    x_ref, x_rows, cap_t, y_edges, y_pad, inside = call(
        factor_lines_x,
        (coefs, SUB, ROWS, ROWS, SUB, 2),
        (cap, warm, v_t, warm_t, source_patch_bits),
    )
    inside = lax.ppermute(inside, "gy", [(i, i ^ 1) for i in range(COUNT_Y)])
    y_ref, y_rows = call(factor_lines_y, (coefs, SUB), (cap_t, y_edges, y_pad))
    s, f, sent, y_high = call(
        begin,
        (ROWS, ROWS, SUB, 1),
        (v_t, warm_t, cap_t, load, inside, outside, y_edges, y_pad, x_ref, x_rows),
        scratch=(ROWS,),
    )
    joined = COUNT_X * SUB
    x_join, s, f, sent = call(
        first_x,
        (SUB * X_COEFS, ROWS, ROWS, SUB),
        (sent, *share_x(sent), cap, load, s, f, x_ref, y_ref, y_rows, y_high),
        scratch=(joined, ROWS),
    )
    y_join, s, f, sent = call(
        first_y,
        (SUB * Y_COEFS, ROWS, ROWS, 2),
        (share_y(sent), cap_t, load, s, f, y_ref, x_ref),
        scratch=(2 * Y_DEPTH * SUB, ROWS),
    )
    f, sent = call(
        second_x,
        (ROWS, 2),
        (sent, *share_x(sent), cap, load, s, f, x_ref, y_ref, x_join),
        scratch=(joined, ROWS),
    )
    (drop,) = call(
        second_y,
        (ROWS,),
        (share_y(sent), f, y_ref, y_join),
        scratch=(2 * Y_DEPTH * SUB, ROWS),
        near=False,
    )
    return drop


def solution(mesh):
    return jax.shard_map(
        local,
        mesh=mesh,
        in_specs=(P("gx", "gy"), P("gx", "gy"), P("gx", "gy"), P(None, "gx", "gy"), P("gx", "gy")),
        out_specs=P("gx", "gy"),
        check_vma=False,
    )
```

```python
import jax
import jax.numpy as jnp
from jax import lax
from jax.experimental import pallas as pl
from jax.experimental.pallas import tpu as pltpu
from jax.sharding import PartitionSpec as P

PITCH = 32
xward_admittance = 1.0
yward_admittance = 0.5
warmth_scaling = 0.004
surrounding_warmth = 25.0
cushion_pieces = 1.0

SUB = 8
LANES = 128
ROWS = 128
DEPTH = ROWS // SUB
COUNT_X = 4
COUNT_Y = 32
Y_DEPTH = COUNT_Y // SUB

INNER = (
    [(m, m - 1, m + 1) for m in range(1, DEPTH - 2, 2)]
    + [(2, 0, 4), (6, 4, 8), (10, 8, 12), (14, 12, 15)]
    + [(4, 0, 8), (12, 8, 15), (8, 0, 15)]
)
SPANS = (1, 2, 4)
X_TURNS = (1, 3, 2)
LOCAL_COEFS = 3 * (len(INNER) + 1 + len(SPANS))

def path_order(nodes):
    order = []
    while len(nodes) > 1:
        for at in range(1, len(nodes), 2):
            right = nodes[at + 1] if at + 1 < len(nodes) else None
            order.append((nodes[at], nodes[at - 1], right))
        nodes = nodes[::2]
    return order + [(nodes[0], None, None)]


X_ORDER = path_order(list(range(2 * COUNT_X)))
X_COEFS = 3 * len(X_ORDER)
Y_ORDER = [(1, 0, 2), (3, 2, 4), (5, 4, 6), (7, 6, 8), (2, 0, 4), (6, 4, 8), (4, 0, 8)]
Y_SENT = 6
Y_COEFS = 3 * (len(Y_ORDER) + len(SPANS)) + 1


def wire(admittance, warm_a, warm_b):
    return admittance / (1.0 + warmth_scaling * (0.5 * (warm_a + warm_b) - surrounding_warmth))


def sublanes():
    return lax.broadcasted_iota(jnp.int32, (SUB, LANES), 0)


def roll(x, by):
    return pltpu.roll(x, by % SUB, 0)


def spread(row):
    return jnp.broadcast_to(row, (SUB, LANES))


def load_lines(ref):
    return [ref[pl.ds(r, SUB, stride=DEPTH), :] for r in range(DEPTH)]


def store_lines(ref, values):
    for r in range(DEPTH):
        ref[pl.ds(r, SUB, stride=DEPTH), :] = values[r]


def load_regs(ref, count=DEPTH):
    return [ref[pl.ds(SUB * r, SUB), :] for r in range(count)]


def store_regs(ref, values):
    for r, value in enumerate(values):
        ref[pl.ds(SUB * r, SUB), :] = value


def coef(ref, k):
    return [ref[pl.ds(SUB * (3 * k + n), SUB), :] for n in range(3)]


def put_coef(ref, k, values):
    for n, value in enumerate(values):
        ref[pl.ds(SUB * (3 * k + n), SUB), :] = value


def factor_local(ref, ground, edges, across):
    sub = sublanes()
    edges = dict(edges)
    for k, (m, left, right) in enumerate(INNER):
        to_left, to_right = edges[(left, m)], edges[(m, right)]
        inverse = 1.0 / (to_left + to_right + ground[m])
        by_left, by_right = to_left * inverse, to_right * inverse
        ground[left] = ground[left] + by_left * ground[m]
        ground[right] = ground[right] + by_right * ground[m]
        edges[(left, right)] = to_left * by_right
        put_coef(ref, k, (inverse, by_left, by_right))
    own, first, last = edges[(0, DEPTH - 1)], ground[0], ground[DEPTH - 1]
    inside = sub < SUB - 1
    inverse = jnp.where(inside, 1.0 / (own + across + last), 0.0)
    by_left, by_right = own * inverse, across * inverse
    put_coef(ref, len(INNER), (inverse, by_left, by_right))
    edge = jnp.where(inside, own * by_right, own)
    end = roll(last, 1)
    first = first + by_left * last + roll(by_right * last, 1)
    for n, span in enumerate(SPANS):
        chosen = sub % (2 * span) == span
        to_left = roll(edge, span)
        inverse = jnp.where(chosen, 1.0 / (to_left + edge + first), 0.0)
        by_left, by_right = to_left * inverse, edge * inverse
        put_coef(ref, len(INNER) + 1 + n, (inverse, by_left, by_right))
        passed = roll(by_right * first, span)
        end = end + passed
        first = first + roll(by_left * first, -span) + jnp.where(sub == 0, 0.0, passed)
        edge = roll(to_left * by_right, -span)
    return edge[0:1], first[0:1], end[0:1]


def forward_local(ref, f):
    sub = sublanes()
    for k, (m, left, right) in enumerate(INNER):
        _, by_left, by_right = coef(ref, k)
        f[left] = f[left] + by_left * f[m]
        f[right] = f[right] + by_right * f[m]
    first, last = f[0], f[DEPTH - 1]
    _, by_left, by_right = coef(ref, len(INNER))
    end = roll(last, 1)
    first = first + by_left * last + roll(by_right * last, 1)
    for n, span in enumerate(SPANS):
        _, by_left, by_right = coef(ref, len(INNER) + 1 + n)
        passed = roll(by_right * first, span)
        end = end + passed
        first = first + roll(by_left * first, -span) + jnp.where(sub == 0, 0.0, passed)
    f[0] = first
    return first[0:1], end[0:1]


def backward_local(ref, f, first, end):
    sub = sublanes()
    x = jnp.where(sub == 0, first, 0.0)
    for n in range(len(SPANS) - 1, -1, -1):
        span = SPANS[n]
        inverse, by_left, by_right = coef(ref, len(INNER) + 1 + n)
        beyond = roll(jnp.where(sub == 0, end, x), -span)
        found = inverse * f[0] + by_left * roll(x, span) + by_right * beyond
        x = jnp.where(sub % (2 * span) == span, found, x)
    inverse, by_left, by_right = coef(ref, len(INNER))
    found = inverse * f[DEPTH - 1] + by_left * x + by_right * roll(x, -1)
    out = [None] * DEPTH
    out[0] = x
    out[DEPTH - 1] = jnp.where(sub == SUB - 1, end, found)
    for k in range(len(INNER) - 1, -1, -1):
        m, left, right = INNER[k]
        inverse, by_left, by_right = coef(ref, k)
        out[m] = inverse * f[m] + by_left * out[left] + by_right * out[right]
    return out


def put_rows(ref, rows):
    for n, row in enumerate(rows):
        ref[n : n + 1, :] = row


def gather_x(joined, own, others):
    place = lax.axis_index("gx")
    count = own.shape[0]
    joined[pl.ds(pl.multiple_of(place * SUB, SUB), count), :] = own[...]
    for n, other in enumerate(others):
        source = jnp.bitwise_xor(place, X_TURNS[n])
        joined[pl.ds(pl.multiple_of(source * SUB, SUB), count), :] = other[...]


def factor_x(ref, joined):
    def row(p, q):
        return spread(joined[SUB * p + q : SUB * p + q + 1, :])

    ground, edges = {}, {}
    for p in range(COUNT_X):
        ground[2 * p], ground[2 * p + 1] = row(p, 2), row(p, 3)
        edges[(2 * p, 2 * p + 1)] = row(p, 4)
        if p + 1 < COUNT_X:
            edges[(2 * p + 1, 2 * p + 2)] = wire(xward_admittance, row(p, 6), row(p + 1, 5))
    for k, (m, left, right) in enumerate(X_ORDER):
        total = ground[m]
        if left is not None:
            total = total + edges[(left, m)]
        if right is not None:
            total = total + edges[(m, right)]
        inverse = 1.0 / total
        by_left = edges[(left, m)] * inverse if left is not None else inverse
        by_right = edges[(m, right)] * inverse if right is not None else inverse
        if left is not None:
            ground[left] = ground[left] + by_left * ground[m]
        if right is not None:
            ground[right] = ground[right] + by_right * ground[m]
        if left is not None and right is not None:
            edges[(left, right)] = edges[(left, m)] * by_right
        put_coef(ref, k, (inverse, by_left, by_right))


def solve_x(ref, joined):
    f = [
        spread(joined[SUB * (n // 2) + n % 2 : SUB * (n // 2) + n % 2 + 1, :])
        for n in range(2 * COUNT_X)
    ]
    for k, (m, left, right) in enumerate(X_ORDER):
        _, by_left, by_right = coef(ref, k)
        if left is not None:
            f[left] = f[left] + by_left * f[m]
        if right is not None:
            f[right] = f[right] + by_right * f[m]
    x = [None] * len(f)
    for k in range(len(X_ORDER) - 1, -1, -1):
        m, left, right = X_ORDER[k]
        inverse, by_left, by_right = coef(ref, k)
        x[m] = inverse * f[m]
        if left is not None:
            x[m] = x[m] + by_left * x[left]
        if right is not None:
            x[m] = x[m] + by_right * x[right]
    place = lax.axis_index("gx")
    first, end = x[0], x[1]
    for p in range(1, COUNT_X):
        first = jnp.where(place == p, x[2 * p], first)
        end = jnp.where(place == p, x[2 * p + 1], end)
    return first, end


def factor_y(ref, joined):
    sub = sublanes()

    def part(r, q):
        return joined[pl.ds(Y_SENT * r + q, SUB, stride=Y_SENT * Y_DEPTH), :]

    ground, edges = {}, {}
    for r in range(Y_DEPTH):
        ground[2 * r], ground[2 * r + 1] = part(r, 2), part(r, 3)
        edges[(2 * r, 2 * r + 1)], edges[(2 * r + 1, 2 * r + 2)] = part(r, 4), part(r, 5)
    last = 2 * Y_DEPTH
    for k, (m, left, right) in enumerate(Y_ORDER):
        to_left, to_right = edges[(left, m)], edges[(m, right)]
        inverse = 1.0 / (to_left + to_right + ground[m])
        by_left, by_right = to_left * inverse, to_right * inverse
        put_coef(ref, k, (inverse, by_left, by_right))
        ground[left] = ground[left] + by_left * ground[m]
        passed = by_right * ground[m]
        if right == last:
            ground[0] = ground[0] + roll(passed, 1)
        else:
            ground[right] = ground[right] + passed
        edges[(left, right)] = to_left * by_right
    edge, first = edges[(0, last)], ground[0]
    for n, span in enumerate(SPANS):
        chosen = sub % (2 * span) == span
        to_left = roll(edge, span)
        inverse = jnp.where(chosen, 1.0 / (to_left + edge + first), 0.0)
        by_left, by_right = to_left * inverse, edge * inverse
        put_coef(ref, len(Y_ORDER) + n, (inverse, by_left, by_right))
        first = first + roll(by_left * first, -span) + roll(by_right * first, span)
        edge = roll(to_left * by_right, -span)
    ref[pl.ds(SUB * (Y_COEFS - 1), SUB), :] = jnp.where(sub == 0, 1.0 / first, 0.0)


def solve_y(ref, joined, stride, found):
    sub = sublanes()
    last = 2 * Y_DEPTH
    f = [
        joined[pl.ds(stride * (n // 2) + n % 2, SUB, stride=stride * Y_DEPTH), :]
        for n in range(last)
    ]
    for k, (m, left, right) in enumerate(Y_ORDER):
        _, by_left, by_right = coef(ref, k)
        f[left] = f[left] + by_left * f[m]
        if right == last:
            f[0] = f[0] + roll(by_right * f[m], 1)
        else:
            f[right] = f[right] + by_right * f[m]
    first = f[0]
    for n, span in enumerate(SPANS):
        _, by_left, by_right = coef(ref, len(Y_ORDER) + n)
        first = first + roll(by_left * first, -span) + roll(by_right * first, span)
    x0 = ref[pl.ds(SUB * (Y_COEFS - 1), SUB), :] * first
    for n in range(len(SPANS) - 1, -1, -1):
        span = SPANS[n]
        inverse, by_left, by_right = coef(ref, len(Y_ORDER) + n)
        value = inverse * first + by_left * roll(x0, span) + by_right * roll(x0, -span)
        x0 = jnp.where(sub % (2 * span) == span, value, x0)
    x = [x0] + [None] * (last - 1) + [roll(x0, -1)]
    for k in range(len(Y_ORDER) - 1, -1, -1):
        m, left, right = Y_ORDER[k]
        inverse, by_left, by_right = coef(ref, k)
        x[m] = inverse * f[m] + by_left * x[left] + by_right * x[right]
    store_regs(found, x[:last])
    place = lax.axis_index("gy")
    at = lax.rem(place, Y_DEPTH) * (2 * SUB) + lax.div(place, Y_DEPTH)
    return spread(found[pl.ds(at, 1), :]), spread(found[pl.ds(at + SUB, 1), :])


def put_rim(ref, v_t, warm_t, low):
    for n, block in enumerate((v_t, warm_t)):
        ref[n : n + 1, :] = jnp.where(low, block[0:1, :], block[ROWS - 1 : ROWS, :])


def prepare(v, warm, v_t, warm_t, outside):
    v_t[...] = v[...].T
    warm_t[...] = warm[...].T
    put_rim(outside, v_t, warm_t, lax.rem(lax.axis_index("gy"), 2) == 0)


def pads(flags, transposed):
    sub = sublanes()
    lane = lax.broadcasted_iota(jnp.int32, (SUB, LANES), 1)
    out = jnp.zeros((SUB, LANES), jnp.float32)
    for a in range(ROWS // PITCH):
        for b in range(LANES // PITCH):
            row, col = (b, a) if transposed else (a, b)
            flag = spread(flags[row : row + 1, col : col + 1])
            here = (sub == a * (PITCH // DEPTH)) & (lane == b * PITCH)
            out = jnp.where(here & (flag == 1), cushion_pieces, out)
    return out


def put_ends(rows, own, first, end):
    rows[...] = jnp.zeros((SUB, LANES), jnp.float32)
    rows[2:3, :] = first
    rows[3:4, :] = end
    rows[4:5, :] = own


def factor_lines_x(
    cap, warm, v_t, warm_t, flags, x_ref, x_rows, cap_t, y_edges, y_pad, inside
):
    put_rim(inside, v_t, warm_t, lax.rem(lax.axis_index("gy"), 2) == 1)
    cap_t[...] = cap[...].T
    temps = load_lines(warm_t)
    store_regs(
        y_edges,
        [wire(yward_admittance, temps[r], temps[r + 1]) for r in range(DEPTH - 1)]
        + [wire(yward_admittance, temps[DEPTH - 1], roll(temps[0], -1))],
    )
    y_pad[...] = pads(flags, True)
    temps = load_lines(warm)
    edges = {
        (r, r + 1): wire(xward_admittance, temps[r], temps[r + 1]) for r in range(DEPTH - 1)
    }
    across = wire(xward_admittance, temps[DEPTH - 1], roll(temps[0], -1))
    ground = load_lines(cap)
    ground[0] = ground[0] + pads(flags, False)
    put_ends(x_rows, *factor_local(x_ref, ground, edges, across))
    x_rows[5:6, :] = warm[0:1, :]
    x_rows[6:7, :] = warm[ROWS - 1 : ROWS, :]


def factor_lines_y(cap_t, y_edges, y_pad, y_ref, y_rows):
    edges = load_regs(y_edges)
    ground = load_lines(cap_t)
    ground[0] = ground[0] + y_pad[...]
    inner = {(r, r + 1): edges[r] for r in range(DEPTH - 1)}
    put_ends(y_rows, *factor_local(y_ref, ground, inner, edges[DEPTH - 1]))


def begin(
    v_t, warm_t, cap_t, load, inside, outside, y_edges, y_pad, x_ref, x_rows,
    s_out, f_out, sent, y_high, flat,
):
    sub = sublanes()
    place = lax.axis_index("gy")
    odd = lax.rem(place, 2) == 1
    low_v = jnp.where(odd, inside[0:1, :], outside[0:1, :])
    low_warm = jnp.where(odd, inside[1:2, :], outside[1:2, :])
    high_v = jnp.where(odd, outside[0:1, :], inside[0:1, :])
    high_warm = jnp.where(odd, outside[1:2, :], inside[1:2, :])
    low_edge = wire(yward_admittance, low_warm, warm_t[0:1, :])
    high_edge = wire(yward_admittance, warm_t[ROWS - 1 : ROWS, :], high_warm)
    low_edge = jnp.where(place > 0, low_edge, 0.0)
    high_edge = jnp.where(place < COUNT_Y - 1, high_edge, 0.0)
    y_high[...] = high_edge
    v = load_lines(v_t)
    cap = load_lines(cap_t)
    edges = load_regs(y_edges)
    before = jnp.where(sub == 0, spread(low_v), roll(v[DEPTH - 1], 1))
    before_edge = jnp.where(sub == 0, spread(low_edge), roll(edges[DEPTH - 1], 1))
    after = jnp.where(sub == SUB - 1, spread(high_v), roll(v[0], -1))
    edges[DEPTH - 1] = jnp.where(sub == SUB - 1, spread(high_edge), edges[DEPTH - 1])
    flow = before_edge * (before - v[0])
    out = []
    for r in range(DEPTH):
        onward = edges[r] * ((v[r + 1] if r + 1 < DEPTH else after) - v[r])
        own = cap[r] * v[r]
        if r == 0:
            own = own - y_pad[...] * v[r]
        out.append(own + (flow + onward))
        flow = -onward
    store_lines(flat, out)
    flat[...] = flat[...].T + load[0]
    s = load_lines(flat)
    store_regs(s_out, s)
    first, end = forward_local(x_ref, s)
    store_regs(f_out, s)
    sent[...] = x_rows[...]
    sent[0:1, :] = first
    sent[1:2, :] = end


def across_x(
    own, one, two, three, cap, load, step, s_in, f_in, x_ref, y_ref, x_join, s_out, f_out, joined, flat
):
    first, end = solve_x(x_join, joined)
    half = backward_local(x_ref, load_regs(f_in), first, end)
    caps, source = load_lines(cap), load_regs(s_in)
    loads = load_lines(load.at[step])
    store_lines(
        flat, [2.0 * caps[r] * half[r] - source[r] + loads[r] for r in range(DEPTH)]
    )
    flat[...] = flat[...].T
    s = load_lines(flat)
    if s_out is not None:
        store_regs(s_out, s)
    ends = forward_local(y_ref, s)
    store_regs(f_out, s)
    return ends


def first_x(
    own, one, two, three, cap, load, s_in, f_in, x_ref, y_ref, y_rows, y_high,
    x_join, s_out, f_out, sent, joined, flat,
):
    gather_x(joined, own, (one, two, three))
    factor_x(x_join, joined)
    first, end = across_x(
        own, one, two, three, cap, load, 0, s_in, f_in, x_ref, y_ref, x_join, s_out, f_out, joined, flat
    )
    rows = [first, end, y_rows[2:3, :], y_rows[3:4, :], y_rows[4:5, :], y_high[...]]
    for n, row in enumerate(rows):
        sent[:, n * LANES : (n + 1) * LANES] = row


def second_x(
    own, one, two, three, cap, load, s_in, f_in, x_ref, y_ref, x_join, f_out, sent, joined, flat
):
    gather_x(joined, own, (one, two, three))
    first, end = across_x(
        own, one, two, three, cap, load, 1, s_in, f_in, x_ref, y_ref, x_join, None, f_out, joined, flat
    )
    sent[0:1, :] = first
    sent[1:2, :] = end


def first_y(
    joined, cap_t, load, s_in, f_in, y_ref, x_ref, y_join, s_out, f_out, sent, found, flat
):
    factor_y(y_join, joined)
    first, end = solve_y(y_join, joined, Y_SENT, found)
    drop = backward_local(y_ref, load_regs(f_in), first, end)
    caps, source = load_lines(cap_t), load_regs(s_in)
    store_lines(flat, [2.0 * caps[r] * drop[r] - source[r] for r in range(DEPTH)])
    flat[...] = flat[...].T + load[1]
    s = load_lines(flat)
    store_regs(s_out, s)
    first, end = forward_local(x_ref, s)
    store_regs(f_out, s)
    sent[0:1, :] = first
    sent[1:2, :] = end


def second_y(joined, f_in, y_ref, y_join, out, found, flat):
    first, end = solve_y(y_join, joined, 2, found)
    store_lines(flat, backward_local(y_ref, load_regs(f_in), first, end))
    out[...] = flat[...].T


def call(body, shapes, args, scratch=(), fetched=True, near=True):
    if fetched:
        args = [pltpu.with_memory_space_constraint(x, pltpu.VMEM) for x in args]
    made = pltpu.VMEM if near else jax.ShapeDtypeStruct
    return pl.pallas_call(
        body,
        out_shape=[
            made(rows if isinstance(rows, tuple) else (rows, LANES), jnp.float32) for rows in shapes
        ],
        in_specs=[pl.BlockSpec(memory_space=pltpu.VMEM)] * len(args),
        out_specs=[pl.BlockSpec(memory_space=pltpu.VMEM)] * len(shapes),
        scratch_shapes=[pltpu.VMEM((rows, LANES), jnp.float32) for rows in scratch],
        name=body.__name__,
    )(*args)


def share_x(sent):
    return [
        lax.ppermute(sent, "gx", [(i, i ^ by) for i in range(COUNT_X)])
        for by in X_TURNS
    ]


def share_y(sent):
    rows = sent.size // LANES
    copies = jnp.broadcast_to(sent[None], (COUNT_Y, *sent.shape))
    return lax.all_to_all(copies, "gy", split_axis=0, concat_axis=0, tiled=True).reshape(
        COUNT_Y * rows, LANES
    )


def outside_pairs():
    pairs = []
    for x in range(COUNT_X):
        for y in range(COUNT_Y):
            if y in (0, COUNT_Y - 1):
                to = ((x ^ 1), y)
            else:
                to = (x, y + 1 if y % 2 else y - 1)
            pairs.append((x * COUNT_Y + y, to[0] * COUNT_Y + to[1]))
    return pairs


def local(starting_sag, warmth_celsius_field, junction_charge_store, load_amperes, source_patch_bits):
    v, warm, cap, load = starting_sag, warmth_celsius_field, junction_charge_store, load_amperes
    v_t, warm_t, outside = call(prepare, (ROWS, ROWS, 2), (v, warm), fetched=False)
    outside = lax.ppermute(outside, ("gx", "gy"), outside_pairs())
    coefs = SUB * LOCAL_COEFS
    x_ref, x_rows, cap_t, y_edges, y_pad, inside = call(
        factor_lines_x,
        (coefs, SUB, ROWS, ROWS, SUB, 2),
        (cap, warm, v_t, warm_t, source_patch_bits),
    )
    inside = lax.ppermute(inside, "gy", [(i, i ^ 1) for i in range(COUNT_Y)])
    y_ref, y_rows = call(factor_lines_y, (coefs, SUB), (cap_t, y_edges, y_pad))
    s, f, sent, y_high = call(
        begin,
        (ROWS, ROWS, SUB, 1),
        (v_t, warm_t, cap_t, load, inside, outside, y_edges, y_pad, x_ref, x_rows),
        scratch=(ROWS,),
    )
    joined = COUNT_X * SUB
    x_join, s, f, sent = call(
        first_x,
        (SUB * X_COEFS, ROWS, ROWS, (1, Y_SENT * LANES)),
        (sent, *share_x(sent), cap, load, s, f, x_ref, y_ref, y_rows, y_high),
        scratch=(joined, ROWS),
    )
    y_join, s, f, sent = call(
        first_y,
        (SUB * Y_COEFS, ROWS, ROWS, 2),
        (share_y(sent), cap_t, load, s, f, y_ref, x_ref),
        scratch=(2 * Y_DEPTH * SUB, ROWS),
    )
    f, sent = call(
        second_x,
        (ROWS, 2),
        (sent, *share_x(sent), cap, load, s, f, x_ref, y_ref, x_join),
        scratch=(joined, ROWS),
    )
    (drop,) = call(
        second_y,
        (ROWS,),
        (share_y(sent), f, y_ref, y_join),
        scratch=(2 * Y_DEPTH * SUB, ROWS),
        near=False,
    )
    return drop


def solution(mesh):
    return jax.shard_map(
        local,
        mesh=mesh,
        in_specs=(P("gx", "gy"), P("gx", "gy"), P("gx", "gy"), P(None, "gx", "gy"), P("gx", "gy")),
        out_specs=P("gx", "gy"),
        check_vma=False,
    )
```

```python
import jax
import jax.numpy as jnp
from jax import lax
from jax.experimental import pallas as pl
from jax.experimental.pallas import tpu as pltpu
from jax.sharding import PartitionSpec as P

PITCH = 32
xward_admittance = 1.0
yward_admittance = 0.5
warmth_scaling = 0.004
surrounding_warmth = 25.0
cushion_pieces = 1.0

SUB = 8
LANES = 128
ROWS = 128
DEPTH = ROWS // SUB
COUNT_X = 4
COUNT_Y = 32
Y_DEPTH = COUNT_Y // SUB

INNER = (
    [(m, m - 1, m + 1) for m in range(1, DEPTH - 2, 2)]
    + [(2, 0, 4), (6, 4, 8), (10, 8, 12), (14, 12, 15)]
    + [(4, 0, 8), (12, 8, 15), (8, 0, 15)]
)
SPANS = (1, 2, 4)
X_TURNS = (1, 3, 2)
LOCAL_COEFS = 3 * (len(INNER) + 1 + len(SPANS))

def path_order(nodes):
    order = []
    while len(nodes) > 1:
        for at in range(1, len(nodes), 2):
            right = nodes[at + 1] if at + 1 < len(nodes) else None
            order.append((nodes[at], nodes[at - 1], right))
        nodes = nodes[::2]
    return order + [(nodes[0], None, None)]


X_ORDER = path_order(list(range(2 * COUNT_X)))
X_COEFS = 3 * len(X_ORDER)
Y_ORDER = [(1, 0, 2), (3, 2, 4), (2, 0, 4)]
Y_SENT = 5
Y_COEFS = 3 * (len(Y_ORDER) + len(SPANS)) + 1


def wire(admittance, warm_a, warm_b):
    return admittance / (1.0 + warmth_scaling * (0.5 * (warm_a + warm_b) - surrounding_warmth))


def sublanes():
    return lax.broadcasted_iota(jnp.int32, (SUB, LANES), 0)


def roll(x, by):
    return pltpu.roll(x, by % SUB, 0)


def spread(row):
    return jnp.broadcast_to(row, (SUB, LANES))


def load_lines(ref):
    return [ref[pl.ds(r, SUB, stride=DEPTH), :] for r in range(DEPTH)]


def store_lines(ref, values):
    for r in range(DEPTH):
        ref[pl.ds(r, SUB, stride=DEPTH), :] = values[r]


def load_regs(ref, count=DEPTH):
    return [ref[pl.ds(SUB * r, SUB), :] for r in range(count)]


def store_regs(ref, values):
    for r, value in enumerate(values):
        ref[pl.ds(SUB * r, SUB), :] = value


def coef(ref, k):
    return [ref[pl.ds(SUB * (3 * k + n), SUB), :] for n in range(3)]


def put_coef(ref, k, values):
    for n, value in enumerate(values):
        ref[pl.ds(SUB * (3 * k + n), SUB), :] = value


def factor_local(ref, ground, edges, across):
    sub = sublanes()
    edges = dict(edges)
    for k, (m, left, right) in enumerate(INNER):
        to_left, to_right = edges[(left, m)], edges[(m, right)]
        inverse = 1.0 / (to_left + to_right + ground[m])
        by_left, by_right = to_left * inverse, to_right * inverse
        ground[left] = ground[left] + by_left * ground[m]
        ground[right] = ground[right] + by_right * ground[m]
        edges[(left, right)] = to_left * by_right
        put_coef(ref, k, (inverse, by_left, by_right))
    own, first, last = edges[(0, DEPTH - 1)], ground[0], ground[DEPTH - 1]
    inside = sub < SUB - 1
    inverse = jnp.where(inside, 1.0 / (own + across + last), 0.0)
    by_left, by_right = own * inverse, across * inverse
    put_coef(ref, len(INNER), (inverse, by_left, by_right))
    edge = jnp.where(inside, own * by_right, own)
    end = roll(last, 1)
    first = first + by_left * last + roll(by_right * last, 1)
    for n, span in enumerate(SPANS):
        chosen = sub % (2 * span) == span
        to_left = roll(edge, span)
        inverse = jnp.where(chosen, 1.0 / (to_left + edge + first), 0.0)
        by_left, by_right = to_left * inverse, edge * inverse
        put_coef(ref, len(INNER) + 1 + n, (inverse, by_left, by_right))
        passed = roll(by_right * first, span)
        end = end + passed
        first = first + roll(by_left * first, -span) + jnp.where(sub == 0, 0.0, passed)
        edge = roll(to_left * by_right, -span)
    return edge[0:1], first[0:1], end[0:1]


def forward_local(ref, f):
    sub = sublanes()
    for k, (m, left, right) in enumerate(INNER):
        _, by_left, by_right = coef(ref, k)
        f[left] = f[left] + by_left * f[m]
        f[right] = f[right] + by_right * f[m]
    first, last = f[0], f[DEPTH - 1]
    _, by_left, by_right = coef(ref, len(INNER))
    end = roll(last, 1)
    first = first + by_left * last + roll(by_right * last, 1)
    for n, span in enumerate(SPANS):
        _, by_left, by_right = coef(ref, len(INNER) + 1 + n)
        passed = roll(by_right * first, span)
        end = end + passed
        first = first + roll(by_left * first, -span) + jnp.where(sub == 0, 0.0, passed)
    f[0] = first
    return first[0:1], end[0:1]


def backward_local(ref, f, first, end):
    sub = sublanes()
    x = jnp.where(sub == 0, first, 0.0)
    for n in range(len(SPANS) - 1, -1, -1):
        span = SPANS[n]
        inverse, by_left, by_right = coef(ref, len(INNER) + 1 + n)
        beyond = roll(jnp.where(sub == 0, end, x), -span)
        found = inverse * f[0] + by_left * roll(x, span) + by_right * beyond
        x = jnp.where(sub % (2 * span) == span, found, x)
    inverse, by_left, by_right = coef(ref, len(INNER))
    found = inverse * f[DEPTH - 1] + by_left * x + by_right * roll(x, -1)
    out = [None] * DEPTH
    out[0] = x
    out[DEPTH - 1] = jnp.where(sub == SUB - 1, end, found)
    for k in range(len(INNER) - 1, -1, -1):
        m, left, right = INNER[k]
        inverse, by_left, by_right = coef(ref, k)
        out[m] = inverse * f[m] + by_left * out[left] + by_right * out[right]
    return out


def put_rows(ref, rows):
    for n, row in enumerate(rows):
        ref[n : n + 1, :] = row


def gather_x(joined, own, others):
    place = lax.axis_index("gx")
    count = own.shape[0]
    joined[pl.ds(pl.multiple_of(place * SUB, SUB), count), :] = own[...]
    for n, other in enumerate(others):
        source = jnp.bitwise_xor(place, X_TURNS[n])
        joined[pl.ds(pl.multiple_of(source * SUB, SUB), count), :] = other[...]


def factor_x(ref, joined):
    def row(p, q):
        return spread(joined[SUB * p + q : SUB * p + q + 1, :])

    ground, edges = {}, {}
    for p in range(COUNT_X):
        ground[2 * p], ground[2 * p + 1] = row(p, 2), row(p, 3)
        edges[(2 * p, 2 * p + 1)] = row(p, 4)
        if p + 1 < COUNT_X:
            edges[(2 * p + 1, 2 * p + 2)] = wire(xward_admittance, row(p, 6), row(p + 1, 5))
    for k, (m, left, right) in enumerate(X_ORDER):
        total = ground[m]
        if left is not None:
            total = total + edges[(left, m)]
        if right is not None:
            total = total + edges[(m, right)]
        inverse = 1.0 / total
        by_left = edges[(left, m)] * inverse if left is not None else inverse
        by_right = edges[(m, right)] * inverse if right is not None else inverse
        if left is not None:
            ground[left] = ground[left] + by_left * ground[m]
        if right is not None:
            ground[right] = ground[right] + by_right * ground[m]
        if left is not None and right is not None:
            edges[(left, right)] = edges[(left, m)] * by_right
        put_coef(ref, k, (inverse, by_left, by_right))


def solve_x(ref, joined):
    f = [
        spread(joined[SUB * (n // 2) + n % 2 : SUB * (n // 2) + n % 2 + 1, :])
        for n in range(2 * COUNT_X)
    ]
    for k, (m, left, right) in enumerate(X_ORDER):
        _, by_left, by_right = coef(ref, k)
        if left is not None:
            f[left] = f[left] + by_left * f[m]
        if right is not None:
            f[right] = f[right] + by_right * f[m]
    x = [None] * len(f)
    for k in range(len(X_ORDER) - 1, -1, -1):
        m, left, right = X_ORDER[k]
        inverse, by_left, by_right = coef(ref, k)
        x[m] = inverse * f[m]
        if left is not None:
            x[m] = x[m] + by_left * x[left]
        if right is not None:
            x[m] = x[m] + by_right * x[right]
    place = lax.axis_index("gx")
    first, end = x[0], x[1]
    for p in range(1, COUNT_X):
        first = jnp.where(place == p, x[2 * p], first)
        end = jnp.where(place == p, x[2 * p + 1], end)
    return first, end


def factor_y(ref, joined):
    sub = sublanes()

    def part(r, q):
        return joined[pl.ds(Y_SENT * r + q, SUB, stride=Y_SENT * Y_DEPTH), :]

    ground, edges = {}, {}
    for r in range(Y_DEPTH):
        passed = part(r - 1, 3) if r > 0 else roll(part(Y_DEPTH - 1, 3), 1)
        ground[r] = part(r, 2) + passed
        edges[(r, r + 1)] = part(r, 4)
    last = Y_DEPTH
    for k, (m, left, right) in enumerate(Y_ORDER):
        to_left, to_right = edges[(left, m)], edges[(m, right)]
        inverse = 1.0 / (to_left + to_right + ground[m])
        by_left, by_right = to_left * inverse, to_right * inverse
        put_coef(ref, k, (inverse, by_left, by_right))
        ground[left] = ground[left] + by_left * ground[m]
        passed = by_right * ground[m]
        if right == last:
            ground[0] = ground[0] + roll(passed, 1)
        else:
            ground[right] = ground[right] + passed
        edges[(left, right)] = to_left * by_right
    edge, first = edges[(0, last)], ground[0]
    for n, span in enumerate(SPANS):
        chosen = sub % (2 * span) == span
        to_left = roll(edge, span)
        inverse = jnp.where(chosen, 1.0 / (to_left + edge + first), 0.0)
        by_left, by_right = to_left * inverse, edge * inverse
        put_coef(ref, len(Y_ORDER) + n, (inverse, by_left, by_right))
        first = first + roll(by_left * first, -span) + roll(by_right * first, span)
        edge = roll(to_left * by_right, -span)
    ref[pl.ds(SUB * (Y_COEFS - 1), SUB), :] = jnp.where(sub == 0, 1.0 / first, 0.0)


def solve_y(ref, joined, stride, link, held, found):
    sub = sublanes()
    last = Y_DEPTH

    def part(r, q):
        return joined[pl.ds(stride * r + q, SUB, stride=stride * Y_DEPTH), :]

    f = []
    for r in range(Y_DEPTH):
        passed = part(r - 1, 1) if r > 0 else roll(part(Y_DEPTH - 1, 1), 1)
        f.append(part(r, 0) + passed)
    for k, (m, left, right) in enumerate(Y_ORDER):
        _, by_left, by_right = coef(ref, k)
        f[left] = f[left] + by_left * f[m]
        if right == last:
            f[0] = f[0] + roll(by_right * f[m], 1)
        else:
            f[right] = f[right] + by_right * f[m]
    first = f[0]
    for n, span in enumerate(SPANS):
        _, by_left, by_right = coef(ref, len(Y_ORDER) + n)
        first = first + roll(by_left * first, -span) + roll(by_right * first, span)
    x0 = ref[pl.ds(SUB * (Y_COEFS - 1), SUB), :] * first
    for n in range(len(SPANS) - 1, -1, -1):
        span = SPANS[n]
        inverse, by_left, by_right = coef(ref, len(Y_ORDER) + n)
        value = inverse * first + by_left * roll(x0, span) + by_right * roll(x0, -span)
        x0 = jnp.where(sub % (2 * span) == span, value, x0)
    x = [x0] + [None] * (last - 1) + [roll(x0, -1)]
    for k in range(len(Y_ORDER) - 1, -1, -1):
        m, left, right = Y_ORDER[k]
        inverse, by_left, by_right = coef(ref, k)
        x[m] = inverse * f[m] + by_left * x[left] + by_right * x[right]
    store_regs(found, x[:last])
    place = lax.axis_index("gy")
    rows = []
    for at in (place, lax.rem(place + 1, COUNT_Y)):
        at = lax.rem(at, Y_DEPTH) * SUB + lax.div(at, Y_DEPTH)
        rows.append(found[pl.ds(at, 1), :])
    first, beyond = rows
    end = link[0:1, :] * held[...] + link[1:2, :] * first + link[2:3, :] * beyond
    return spread(first), spread(end)


def put_rim(ref, v_t, warm_t, low):
    for n, block in enumerate((v_t, warm_t)):
        ref[n : n + 1, :] = jnp.where(low, block[0:1, :], block[ROWS - 1 : ROWS, :])


def prepare(v, warm, v_t, warm_t, outside):
    v_t[...] = v[...].T
    warm_t[...] = warm[...].T
    put_rim(outside, v_t, warm_t, lax.rem(lax.axis_index("gy"), 2) == 0)


def pads(flags, transposed):
    sub = sublanes()
    lane = lax.broadcasted_iota(jnp.int32, (SUB, LANES), 1)
    out = jnp.zeros((SUB, LANES), jnp.float32)
    for a in range(ROWS // PITCH):
        for b in range(LANES // PITCH):
            row, col = (b, a) if transposed else (a, b)
            flag = spread(flags[row : row + 1, col : col + 1])
            here = (sub == a * (PITCH // DEPTH)) & (lane == b * PITCH)
            out = jnp.where(here & (flag == 1), cushion_pieces, out)
    return out


def put_ends(rows, own, first, end):
    rows[...] = jnp.zeros((SUB, LANES), jnp.float32)
    rows[2:3, :] = first
    rows[3:4, :] = end
    rows[4:5, :] = own


def factor_lines_x(
    cap, warm, v_t, warm_t, flags, x_ref, x_rows, cap_t, y_edges, y_pad, inside
):
    put_rim(inside, v_t, warm_t, lax.rem(lax.axis_index("gy"), 2) == 1)
    cap_t[...] = cap[...].T
    temps = load_lines(warm_t)
    store_regs(
        y_edges,
        [wire(yward_admittance, temps[r], temps[r + 1]) for r in range(DEPTH - 1)]
        + [wire(yward_admittance, temps[DEPTH - 1], roll(temps[0], -1))],
    )
    y_pad[...] = pads(flags, True)
    temps = load_lines(warm)
    edges = {
        (r, r + 1): wire(xward_admittance, temps[r], temps[r + 1]) for r in range(DEPTH - 1)
    }
    across = wire(xward_admittance, temps[DEPTH - 1], roll(temps[0], -1))
    ground = load_lines(cap)
    ground[0] = ground[0] + pads(flags, False)
    put_ends(x_rows, *factor_local(x_ref, ground, edges, across))
    x_rows[5:6, :] = warm[0:1, :]
    x_rows[6:7, :] = warm[ROWS - 1 : ROWS, :]


def factor_lines_y(cap_t, y_edges, y_pad, y_ref, y_rows):
    edges = load_regs(y_edges)
    ground = load_lines(cap_t)
    ground[0] = ground[0] + y_pad[...]
    inner = {(r, r + 1): edges[r] for r in range(DEPTH - 1)}
    put_ends(y_rows, *factor_local(y_ref, ground, inner, edges[DEPTH - 1]))


def begin(
    v_t, warm_t, cap_t, load, inside, outside, y_edges, y_pad, x_ref, x_rows,
    s_out, f_out, sent, y_high, flat,
):
    sub = sublanes()
    place = lax.axis_index("gy")
    odd = lax.rem(place, 2) == 1
    low_v = jnp.where(odd, inside[0:1, :], outside[0:1, :])
    low_warm = jnp.where(odd, inside[1:2, :], outside[1:2, :])
    high_v = jnp.where(odd, outside[0:1, :], inside[0:1, :])
    high_warm = jnp.where(odd, outside[1:2, :], inside[1:2, :])
    low_edge = wire(yward_admittance, low_warm, warm_t[0:1, :])
    high_edge = wire(yward_admittance, warm_t[ROWS - 1 : ROWS, :], high_warm)
    low_edge = jnp.where(place > 0, low_edge, 0.0)
    high_edge = jnp.where(place < COUNT_Y - 1, high_edge, 0.0)
    y_high[...] = high_edge
    v = load_lines(v_t)
    cap = load_lines(cap_t)
    edges = load_regs(y_edges)
    before = jnp.where(sub == 0, spread(low_v), roll(v[DEPTH - 1], 1))
    before_edge = jnp.where(sub == 0, spread(low_edge), roll(edges[DEPTH - 1], 1))
    after = jnp.where(sub == SUB - 1, spread(high_v), roll(v[0], -1))
    edges[DEPTH - 1] = jnp.where(sub == SUB - 1, spread(high_edge), edges[DEPTH - 1])
    flow = before_edge * (before - v[0])
    out = []
    for r in range(DEPTH):
        onward = edges[r] * ((v[r + 1] if r + 1 < DEPTH else after) - v[r])
        own = cap[r] * v[r]
        if r == 0:
            own = own - y_pad[...] * v[r]
        out.append(own + (flow + onward))
        flow = -onward
    store_lines(flat, out)
    flat[...] = flat[...].T + load[0]
    s = load_lines(flat)
    store_regs(s_out, s)
    first, end = forward_local(x_ref, s)
    store_regs(f_out, s)
    sent[...] = x_rows[...]
    sent[0:1, :] = first
    sent[1:2, :] = end


def across_x(
    own, one, two, three, cap, load, step, s_in, f_in, x_ref, y_ref, x_join, s_out, f_out, joined, flat
):
    first, end = solve_x(x_join, joined)
    half = backward_local(x_ref, load_regs(f_in), first, end)
    caps, source = load_lines(cap), load_regs(s_in)
    loads = load_lines(load.at[step])
    store_lines(
        flat, [2.0 * caps[r] * half[r] - source[r] + loads[r] for r in range(DEPTH)]
    )
    flat[...] = flat[...].T
    s = load_lines(flat)
    if s_out is not None:
        store_regs(s_out, s)
    ends = forward_local(y_ref, s)
    store_regs(f_out, s)
    return ends


def first_x(
    own, one, two, three, cap, load, s_in, f_in, x_ref, y_ref, y_rows, y_high,
    x_join, s_out, f_out, sent, link, held, joined, flat,
):
    gather_x(joined, own, (one, two, three))
    factor_x(x_join, joined)
    first, end = across_x(
        own, one, two, three, cap, load, 0, s_in, f_in, x_ref, y_ref, x_join, s_out, f_out, joined, flat
    )
    own, across, end_ground = y_rows[4:5, :], y_high[...], y_rows[3:4, :]
    inverse = 1.0 / (own + across + end_ground)
    by_left, by_right = own * inverse, across * inverse
    put_rows(link, [inverse, by_left, by_right])
    held[...] = end
    rows = [first + by_left * end, by_right * end]
    rows += [y_rows[2:3, :] + by_left * end_ground, by_right * end_ground, own * by_right]
    for n, row in enumerate(rows):
        sent[:, n * LANES : (n + 1) * LANES] = row


def second_x(
    own, one, two, three, cap, load, s_in, f_in, x_ref, y_ref, x_join, link, f_out, sent, held, joined, flat
):
    gather_x(joined, own, (one, two, three))
    first, end = across_x(
        own, one, two, three, cap, load, 1, s_in, f_in, x_ref, y_ref, x_join, None, f_out, joined, flat
    )
    held[...] = end
    put_rows(sent, [first + link[1:2, :] * end, link[2:3, :] * end])


def first_y(
    joined, cap_t, load, s_in, f_in, y_ref, x_ref, link, held, y_join, s_out, f_out, sent, found, flat
):
    factor_y(y_join, joined)
    first, end = solve_y(y_join, joined, Y_SENT, link, held, found)
    drop = backward_local(y_ref, load_regs(f_in), first, end)
    caps, source = load_lines(cap_t), load_regs(s_in)
    store_lines(flat, [2.0 * caps[r] * drop[r] - source[r] for r in range(DEPTH)])
    flat[...] = flat[...].T + load[1]
    s = load_lines(flat)
    store_regs(s_out, s)
    first, end = forward_local(x_ref, s)
    store_regs(f_out, s)
    sent[0:1, :] = first
    sent[1:2, :] = end


def second_y(joined, f_in, y_ref, y_join, link, held, out, found, flat):
    first, end = solve_y(y_join, joined, 2, link, held, found)
    store_lines(flat, backward_local(y_ref, load_regs(f_in), first, end))
    out[...] = flat[...].T


def call(body, shapes, args, scratch=(), fetched=True, near=True):
    if fetched:
        args = [pltpu.with_memory_space_constraint(x, pltpu.VMEM) for x in args]
    made = pltpu.VMEM if near else jax.ShapeDtypeStruct
    return pl.pallas_call(
        body,
        out_shape=[
            made(rows if isinstance(rows, tuple) else (rows, LANES), jnp.float32) for rows in shapes
        ],
        in_specs=[pl.BlockSpec(memory_space=pltpu.VMEM)] * len(args),
        out_specs=[pl.BlockSpec(memory_space=pltpu.VMEM)] * len(shapes),
        scratch_shapes=[pltpu.VMEM((rows, LANES), jnp.float32) for rows in scratch],
        name=body.__name__,
    )(*args)


def share_x(sent):
    return [
        lax.ppermute(sent, "gx", [(i, i ^ by) for i in range(COUNT_X)])
        for by in X_TURNS
    ]


def share_y(sent):
    rows = sent.size // LANES
    copies = jnp.broadcast_to(sent[None], (COUNT_Y, *sent.shape))
    return lax.all_to_all(copies, "gy", split_axis=0, concat_axis=0, tiled=True).reshape(
        COUNT_Y * rows, LANES
    )


def outside_pairs():
    pairs = []
    for x in range(COUNT_X):
        for y in range(COUNT_Y):
            if y in (0, COUNT_Y - 1):
                to = ((x ^ 1), y)
            else:
                to = (x, y + 1 if y % 2 else y - 1)
            pairs.append((x * COUNT_Y + y, to[0] * COUNT_Y + to[1]))
    return pairs


def local(starting_sag, warmth_celsius_field, junction_charge_store, load_amperes, source_patch_bits):
    v, warm, cap, load = starting_sag, warmth_celsius_field, junction_charge_store, load_amperes
    v_t, warm_t, outside = call(prepare, (ROWS, ROWS, 2), (v, warm), fetched=False)
    outside = lax.ppermute(outside, ("gx", "gy"), outside_pairs())
    coefs = SUB * LOCAL_COEFS
    x_ref, x_rows, cap_t, y_edges, y_pad, inside = call(
        factor_lines_x,
        (coefs, SUB, ROWS, ROWS, SUB, 2),
        (cap, warm, v_t, warm_t, source_patch_bits),
    )
    inside = lax.ppermute(inside, "gy", [(i, i ^ 1) for i in range(COUNT_Y)])
    y_ref, y_rows = call(factor_lines_y, (coefs, SUB), (cap_t, y_edges, y_pad))
    s, f, sent, y_high = call(
        begin,
        (ROWS, ROWS, SUB, 1),
        (v_t, warm_t, cap_t, load, inside, outside, y_edges, y_pad, x_ref, x_rows),
        scratch=(ROWS,),
    )
    joined = COUNT_X * SUB
    x_join, s, f, sent, link, held = call(
        first_x,
        (SUB * X_COEFS, ROWS, ROWS, (1, Y_SENT * LANES), 3, 1),
        (sent, *share_x(sent), cap, load, s, f, x_ref, y_ref, y_rows, y_high),
        scratch=(joined, ROWS),
    )
    y_join, s, f, sent = call(
        first_y,
        (SUB * Y_COEFS, ROWS, ROWS, 2),
        (share_y(sent), cap_t, load, s, f, y_ref, x_ref, link, held),
        scratch=(Y_DEPTH * SUB, ROWS),
    )
    f, sent, held = call(
        second_x,
        (ROWS, 2, 1),
        (sent, *share_x(sent), cap, load, s, f, x_ref, y_ref, x_join, link),
        scratch=(joined, ROWS),
    )
    (drop,) = call(
        second_y,
        (ROWS,),
        (share_y(sent), f, y_ref, y_join, link, held),
        scratch=(Y_DEPTH * SUB, ROWS),
        near=False,
    )
    return drop


def solution(mesh):
    return jax.shard_map(
        local,
        mesh=mesh,
        in_specs=(P("gx", "gy"), P("gx", "gy"), P("gx", "gy"), P(None, "gx", "gy"), P("gx", "gy")),
        out_specs=P("gx", "gy"),
        check_vma=False,
    )
```
